32 devices in a mesh: groups: 2 (over y), rows: 4 (over z), clips: 2 (over x), frames: 2 (over core).
Axes of the slice: x: 2, y: 2, z: 4, core: 2. Of those that a mesh axis runs over, the one named last changes fastest.
Arguments:
- pixels: bfloat16 [4, 8, 3, 16, 256], P(('groups', 'clips'), 'frames', None, 'rows'), parts along dimension 0, may hold values from -6 to 6
- frame_counts: int32 [4], P(('groups', 'clips')), parts along dimension 0, may hold values from 1 to 8
- weight_first: bfloat16 [3, 3, 3, 64, 3], replicated, may hold values from -0.625 to 0.625
- weight_second: bfloat16 [3, 3, 3, 64, 64], replicated, may hold values from -0.15625 to 0.15625
- weight_down: bfloat16 [3, 3, 64, 64], replicated, may hold values from -0.25 to 0.25
Outputs:
- encoded: bfloat16 [4, 8, 64, 8, 128], P(('groups', 'clips'), 'frames', None, 'rows'), parts along dimension 0
The draws below stay inside these ranges and needn't reach their ends.
There are 2 independent parts, one for each index of `groups`. The reference program is written for one: setup_inputs(seed, part) draws one part's arguments, and reference() takes and returns one part's arrays. A program takes and returns all parts, laid end to end along the dimension named above; an argument that names none is the same for every part. Nothing has to cross between parts.
Inputs may be any that keep to these rules, and one draw needn't show every extreme that they name: `frame_counts`: the number of real frames of each clip; later frame slots are ignored.
All inputs are finite; a program needn't handle non-finite values.
Results may differ from the reference program's by a relative error of at most 0.006.
Values may be sent and summed in bfloat16 or wider, within the bound.
No kernel may reach another device: no remote copies, remote signals or barrier semaphores. Data moves between devices by JAX's collectives and lax.ppermute only.
A program may use at most 64 MiB of HBM per device.

```python
import jax
import jax.numpy as jnp
from jax import lax

CHANNELS = 64
COLORS = 3
WIDTH = 256
CLIPS = 2
TMAX = 8
HEIGHT = 16


def block_levels(rng, shape, cuts, low, high):
    loudness, own = 1.0, jax.random.fold_in(rng, 6)
    for dim, blocks in cuts:
        heights = jnp.exp(jax.random.uniform(jax.random.fold_in(own, dim), (blocks,), jnp.float32, low / len(cuts), high / len(cuts)))
        loudness = loudness * jnp.repeat(heights, shape[dim] // blocks).reshape([-1 if axis == dim else 1 for axis in range(len(shape))])
    return loudness


def scatter_about(key, dims, scale, limit, cuts=(), held_as=jnp.bfloat16):
    level = block_levels(key, dims, cuts, -0.22, 0.18) if cuts else 1.0
    array = jax.random.normal(key, dims, jnp.float32) * scale * level
    return jnp.minimum(jnp.maximum(array, -limit), limit).astype(held_as)


def setup_inputs(seed: int = 0, part: int = 0) -> dict:
    key_of = jax.random.split(jax.random.key(seed), 6)
    part_keys = jax.random.split(jax.random.fold_in(key_of[5], part), 6)
    pixels = scatter_about(part_keys[0], (CLIPS, TMAX, COLORS, HEIGHT, WIDTH), 1.0, 6.0, ((0, 2), (1, 2), (3, 4)))
    frame_counts = jax.random.randint(part_keys[1], (CLIPS,), 1, TMAX + 1).astype(jnp.int32)
    weight_first = scatter_about(key_of[2], (3, 3, 3, CHANNELS, COLORS), (27 * COLORS) ** -0.5, 0.625)
    weight_second = scatter_about(key_of[3], (3, 3, 3, CHANNELS, CHANNELS), (27 * CHANNELS) ** -0.5, 0.15625)
    weight_down = scatter_about(key_of[4], (3, 3, CHANNELS, CHANNELS), (9 * CHANNELS) ** -0.5, 0.25)
    return dict(pixels=pixels, frame_counts=frame_counts, weight_first=weight_first, weight_second=weight_second, weight_down=weight_down)


def conv_block(source, weight, frames, rows):
    width = source.shape[-1]
    padded = jnp.pad(source, ((0, 0), (0, 0), (0, 0), (0, 0), (1, 1)))
    total = jnp.zeros((source.shape[0], frames, weight.shape[3], rows, width), jnp.float32)
    for tap_t in range(3):
        for tap_y in range(3):
            for tap_x in range(3):
                piece = padded[:, tap_t:tap_t + frames, :, tap_y:tap_y + rows, tap_x:tap_x + width]
                total = total + jnp.einsum("oi,ctiyx->ctoyx", weight[tap_t, tap_y, tap_x].astype(jnp.float32), piece.astype(jnp.float32), precision=lax.Precision.HIGHEST)
    return total


def conv_down(source, weight):
    rows = (source.shape[3] - 1) // 2
    width = source.shape[4] // 2
    padded = jnp.pad(source, ((0, 0), (0, 0), (0, 0), (0, 0), (1, 1)))
    total = jnp.zeros((source.shape[0], source.shape[1], weight.shape[2], rows, width), jnp.float32)
    for tap_y in range(3):
        for tap_x in range(3):
            piece = padded[:, :, :, tap_y:tap_y + 2 * rows:2, tap_x:tap_x + 2 * width:2]
            total = total + jnp.einsum("oi,ctiyx->ctoyx", weight[tap_y, tap_x].astype(jnp.float32), piece.astype(jnp.float32), precision=lax.Precision.HIGHEST)
    return total


def reference(pixels, frame_counts, weight_first, weight_second, weight_down):
    def one_clip(item):
        clip, count = item
        clip = clip[None]
        live = (jnp.arange(TMAX, dtype=jnp.int32) < count).astype(jnp.float32)[None, :, None, None, None]
        source = jnp.pad(clip, ((0, 0), (2, 0), (0, 0), (1, 1), (0, 0)))
        first = (conv_block(source, weight_first, TMAX, HEIGHT) * live).astype(jnp.bfloat16)
        act = jax.nn.silu(first.astype(jnp.float32)).astype(jnp.bfloat16)
        act_pad = jnp.pad(act, ((0, 0), (2, 0), (0, 0), (1, 1), (0, 0)))
        second = conv_block(act_pad, weight_second, TMAX, HEIGHT) * live
        summed = (first.astype(jnp.float32) + second).astype(jnp.bfloat16)
        summed_pad = jnp.pad(summed, ((0, 0), (0, 0), (0, 0), (1, 0), (0, 0)))
        return conv_down(summed_pad, weight_down).astype(jnp.bfloat16)[0]

    return lax.map(one_clip, (pixels, frame_counts))
```

```python
import jax
import jax.numpy as jnp
import numpy as np
from jax import lax
from jax.experimental import pallas as pl
from jax.experimental.pallas import tpu as pltpu
from jax.sharding import PartitionSpec as P

VIEWS = 4
PARITIES = 2
TAPS = 3
SLOT = 16

VMEM = pl.BlockSpec(memory_space=pltpu.VMEM)
SMEM = pl.BlockSpec(memory_space=pltpu.SMEM)


def view_columns(width):
    half = width // 2
    select = np.zeros((width, VIEWS * half), np.float32)
    for view in range(VIEWS):
        for x in range(half):
            column = 2 * x + view - 1
            if 0 <= column < width:
                select[column, view * half + x] = 1
    return select


def first_places(rows, colors):
    sources = 3
    places = np.zeros((rows + 3, PARITIES, TAPS, TAPS, TAPS, colors, TAPS, VIEWS, sources, SLOT), np.float32)
    for row in range(rows + 3):
        for tap_y in range(TAPS):
            pixel_row = row + tap_y - 3
            if pixel_row < 0:
                source, local = 1, pixel_row + rows
            elif pixel_row < rows:
                source, local = 0, pixel_row
            else:
                source, local = 2, pixel_row - rows
            for parity in range(PARITIES):
                for tap_t in range(TAPS):
                    for tap_x in range(TAPS):
                        for color in range(colors):
                            places[row, parity, tap_t, tap_y, tap_x, color, tap_t, tap_x + parity, source, color * rows + local] = 1
    return places.reshape((rows + 3) * PARITIES, TAPS**3 * colors, TAPS * VIEWS * sources * SLOT)


def prepare_kernel(first_ref, places_ref, second_ref, down_ref, first_out, second_out, down_out):
    channels = first_ref.shape[0]
    first = first_ref[...]
    for block in range(places_ref.shape[0]):
        placed = jnp.dot(first, places_ref[block], preferred_element_type=jnp.float32)
        first_out[block * channels:(block + 1) * channels, :] = placed.astype(jnp.bfloat16)
    none = jnp.zeros((channels, channels), jnp.bfloat16)
    for tap_t in range(TAPS):
        for tap_y in range(TAPS):
            base = (tap_t * TAPS + tap_y) * TAPS
            taps = [second_ref[base + tap_x] for tap_x in range(TAPS)]
            columns = slice(base // TAPS * VIEWS * channels, (base // TAPS + 1) * VIEWS * channels)
            second_out[:channels, columns] = jnp.concatenate(taps + [none], axis=1)
            second_out[channels:, columns] = jnp.concatenate([none] + taps, axis=1)
    out_rows = down_out.shape[0] // channels
    sum_rows = down_out.shape[1] // (TAPS * channels)
    taps = jnp.concatenate([down_ref[tap] for tap in range(TAPS * TAPS)], axis=1)
    place = lax.broadcasted_iota(jnp.int32, (down_out.shape[0], channels), 0)
    channel = lax.broadcasted_iota(jnp.int32, (down_out.shape[0], channels), 1)
    total = None
    for y in range(out_rows):
        spread = (place == channel * out_rows + y).astype(jnp.float32).astype(jnp.bfloat16)
        pieces = [taps]
        before, after = 2 * y, sum_rows - TAPS - 2 * y
        if before:
            pieces = [jnp.zeros((channels, before * TAPS * channels), jnp.bfloat16)] + pieces
        if after:
            pieces = pieces + [jnp.zeros((channels, after * TAPS * channels), jnp.bfloat16)]
        part = jnp.dot(spread, jnp.concatenate(pieces, axis=1), preferred_element_type=jnp.float32)
        total = part if total is None else total + part
    down_out[...] = total.astype(jnp.bfloat16)


def encode_kernel(count_ref, own_ref, above_ref, below_ref, columns_ref, first_w, second_w, down_w, out_ref, views, act, held, taps, *, rows, frames):
    half = columns_ref.shape[1] // VIEWS
    channels = second_w.shape[0] // PARITIES
    pair = PARITIES * channels
    wide = (frames + 2) * half
    narrow = frames * half
    for source, ref in enumerate((own_ref, above_ref, below_ref)):
        spread = jnp.dot(ref[...], columns_ref[...], preferred_element_type=jnp.float32).astype(jnp.bfloat16)
        for view in range(VIEWS):
            place = (view * 3 + source) * SLOT
            for t in range(frames + 4):
                views[place:place + SLOT, t * half:(t + 1) * half] = spread[t * SLOT:(t + 1) * SLOT, view * half:(view + 1) * half]

    start = lax.axis_index("frames") * frames
    row_start = lax.axis_index("rows") * rows
    height = lax.axis_size("rows") * rows
    slot = lax.broadcasted_iota(jnp.int32, (1, wide), 1)
    live = (slot // half + (start - 2) < count_ref[0]).astype(jnp.float32)
    lane = lax.broadcasted_iota(jnp.int32, (channels, half), 1)
    depth = views.shape[0]
    for row in range(rows + 3):
        inside = jnp.logical_and(row_start + (row - 2) >= 0, row_start + (row - 2) < height).astype(jnp.float32)
        total = None
        for tap in range(TAPS):
            part = jnp.dot(
                first_w[row * pair:(row + 1) * pair, tap * depth:(tap + 1) * depth],
                views[:, tap * half:tap * half + wide],
                preferred_element_type=jnp.float32,
            )
            total = part if total is None else total + part
        first = (total * (live * inside)).astype(jnp.bfloat16)
        if 1 <= row <= rows + 1:
            held[(row - 1) * pair:row * pair, :] = first[:, 2 * half:]
        value = first.astype(jnp.float32)
        value = value / (1 + jnp.exp(-value))
        base = row * VIEWS * channels
        act[base + channels:base + 3 * channels, :] = value.astype(jnp.bfloat16)
        for t in range(frames + 2):
            lanes = slice(t * half, (t + 1) * half)
            left = jnp.where(lane == 0, 0.0, pltpu.roll(value[channels:, lanes], 1, 1))
            right = jnp.where(lane == half - 1, 0.0, pltpu.roll(value[:channels, lanes], half - 1, 1))
            act[base:base + channels, lanes] = left.astype(jnp.bfloat16)
            act[base + 3 * channels:base + 4 * channels, lanes] = right.astype(jnp.bfloat16)

    window = TAPS * VIEWS * channels
    for row in range(rows + 1):
        base = row * VIEWS * channels
        total = None
        for tap in range(TAPS):
            part = jnp.dot(
                second_w[:, tap * window:(tap + 1) * window],
                act[base:base + window, tap * half:tap * half + narrow],
                preferred_element_type=jnp.float32,
            )
            total = part if total is None else total + part
        inside = (row_start + (row - 1) >= 0).astype(jnp.float32)
        second = total * (live[:, 2 * half:] * inside)
        value = (held[row * pair:(row + 1) * pair, :].astype(jnp.float32) + second).astype(jnp.bfloat16)
        base = row * TAPS * channels
        taps[base + channels:base + 3 * channels, :] = value
        value = value.astype(jnp.float32)
        for t in range(frames):
            lanes = slice(t * half, (t + 1) * half)
            left = jnp.where(lane == 0, 0.0, pltpu.roll(value[channels:, lanes], 1, 1))
            taps[base:base + channels, lanes] = left.astype(jnp.bfloat16)
    encoded = jnp.dot(down_w[...], taps[...], preferred_element_type=jnp.float32).astype(jnp.bfloat16)
    size = down_w.shape[0]
    for t in range(frames):
        out_ref[t * size:(t + 1) * size, :] = encoded[:, t * half:(t + 1) * half]


def packed(pixels):
    frames, colors, rows, width = pixels.shape
    flat = pixels.reshape(frames, colors * rows, width)
    return jnp.pad(flat, ((0, 0), (0, SLOT - colors * rows), (0, 0))).reshape(frames * SLOT, width)


def shards(pixels, frame_counts, weight_first, weight_second, weight_down):
    clips, frames, colors, rows, width = pixels.shape
    channels = weight_first.shape[3]
    half = width // 2
    out_rows = rows // 2
    frame_devices, row_devices = lax.axis_size("frames"), lax.axis_size("rows")
    assert clips == 1 and frames >= 4 and rows >= 3 and rows % 2 == 0 and colors * rows <= SLOT
    earlier = lax.ppermute(pixels[:, -4:], "frames", [(i, i + 1) for i in range(frame_devices - 1)])
    own = jnp.concatenate([packed(earlier[0]), packed(pixels[0])], axis=0)
    above = lax.ppermute(own, "rows", [(i, i + 1) for i in range(row_devices - 1)])
    below = lax.ppermute(own, "rows", [(i + 1, i) for i in range(row_devices - 1)])

    bf16 = jnp.bfloat16
    places = jnp.asarray(first_places(rows, colors), bf16)
    columns = jnp.asarray(view_columns(width), bf16)
    pair = PARITIES * channels
    first_w, second_w, down_w = pl.pallas_call(
        prepare_kernel,
        name="prepare",
        compiler_params=pltpu.CompilerParams(vmem_limit_bytes=8 << 20),
        in_specs=[VMEM] * 4,
        out_specs=[VMEM] * 3,
        out_shape=[
            jax.ShapeDtypeStruct(((rows + 3) * pair, places.shape[2]), bf16),
            jax.ShapeDtypeStruct((pair, TAPS * TAPS * VIEWS * channels), bf16),
            jax.ShapeDtypeStruct((channels * out_rows, (rows + 1) * TAPS * channels), bf16),
        ],
    )(
        weight_first.transpose(3, 0, 1, 2, 4).reshape(channels, TAPS**3 * colors),
        places,
        weight_second.reshape(TAPS**3, channels, channels),
        weight_down.reshape(TAPS**2, channels, channels),
    )
    wide, narrow = (frames + 2) * half, frames * half
    encoded = pl.pallas_call(
        lambda *refs: encode_kernel(*refs, rows=rows, frames=frames),
        name="encode",
        compiler_params=pltpu.CompilerParams(vmem_limit_bytes=24 << 20),
        in_specs=[SMEM] + [VMEM] * 7,
        out_specs=VMEM,
        out_shape=jax.ShapeDtypeStruct((frames * channels * out_rows, half), bf16),
        scratch_shapes=[
            pltpu.VMEM((VIEWS * 3 * SLOT, (frames + 4) * half), bf16),
            pltpu.VMEM(((rows + 3) * VIEWS * channels, wide), bf16),
            pltpu.VMEM(((rows + 1) * pair, narrow), bf16),
            pltpu.VMEM(((rows + 1) * TAPS * channels, narrow), bf16),
        ],
    )(frame_counts, own, above, below, columns, first_w, second_w, down_w)
    return encoded.reshape(1, frames, channels, out_rows, half)


def solution(mesh):
    in_specs = (
        P(("groups", "clips"), "frames", None, "rows", None),
        P(("groups", "clips")),
        P(),
        P(),
        P(),
    )
    out_specs = P(("groups", "clips"), "frames", None, "rows", None)
    return jax.shard_map(shards, mesh=mesh, in_specs=in_specs, out_specs=out_specs, check_vma=False)
```

```python
import jax
import jax.numpy as jnp
from jax import lax
from jax.experimental import pallas as pl
from jax.experimental.pallas import tpu as pltpu
from jax.sharding import PartitionSpec as P

VIEWS = 4
PARITIES = 2
TAPS = 3
GROUP = 3
SLOT = 16
SUBLANES = 8

VMEM = pl.BlockSpec(memory_space=pltpu.VMEM)
HBM = pl.BlockSpec(memory_space=pltpu.HBM)
SMEM = pl.BlockSpec(memory_space=pltpu.SMEM)


def one_hot(shape, target, valid):
    lane = lax.broadcasted_iota(jnp.int32, shape, 1)
    return jnp.where(lane == jnp.where(valid, target, -1), 1.0, 0.0).astype(jnp.bfloat16)


def prepare_kernel(count, first_hbm, second_hbm, down_hbm, first_out, second_out, down_out, live_out, gather_out, columns_out, first, second, down, sems, *, rows, frames):
    arrays = ((first_hbm, first), (second_hbm, second), (down_hbm, down))
    copies = [pltpu.make_async_copy(source, target, sems.at[i]) for i, (source, target) in enumerate(arrays)]
    for copy in copies:
        copy.start()
    channels = first.shape[2]
    colors = first.shape[1]

    size = TAPS**3 * SUBLANES
    line = lax.broadcasted_iota(jnp.int32, (size, 1), 0)
    tap, color = line // SUBLANES, line % SUBLANES
    target = (tap // TAPS**2 * VIEWS + tap % TAPS) * SLOT + tap // TAPS % TAPS * colors + color
    chosen = one_hot((size, first_out.shape[1]), target, color < colors)

    width = columns_out.shape[0]
    column = lax.broadcasted_iota(jnp.int32, columns_out.shape, 0)
    place = lax.broadcasted_iota(jnp.int32, columns_out.shape, 1)
    half = width // 2
    columns_out[...] = jnp.where(column == place % half * 2 + place // half - 1, 1.0, 0.0).astype(jnp.bfloat16)

    odd = lax.rem(lax.axis_index("frames"), 2)
    groups = -(-(rows + 3) // GROUP)
    line = lax.broadcasted_iota(jnp.int32, (gather_out.shape[0], 1), 0)
    frame, group, inner = line // (groups * SLOT), line // SLOT % groups, line % SLOT
    row, color = group * GROUP + inner // colors - 3, inner % colors
    source = jnp.where(row < 0, 1 + odd, jnp.where(row < rows, 0, 2 - odd))
    local = jnp.where(row < 0, row + rows, jnp.where(row < rows, row, row - rows))
    target = ((source * (frames + 4) + frame) * colors + color) * rows + local
    gather_out[...] = one_hot(gather_out.shape, target, jnp.logical_and(inner < (GROUP + 2) * colors, row < rows + 2))

    half = live_out.shape[1] // (frames + 2)
    frame = lax.broadcasted_iota(jnp.int32, live_out.shape, 1) // half + (lax.axis_index("frames") * frames - 2)
    row = lax.broadcasted_iota(jnp.int32, live_out.shape, 0) + (lax.axis_index("rows") * rows - 2)
    inside = jnp.logical_and(row >= 0, row < lax.axis_size("rows") * rows)
    live_out[...] = jnp.where(jnp.logical_and(inside, frame < count[0]), 1.0, 0.0)

    for copy in copies:
        copy.wait()
    filler = jnp.zeros((SUBLANES - colors, channels), jnp.float32)
    lines = []
    for tap in range(TAPS**3):
        lines += [first[tap].astype(jnp.float32), filler]
    lines = jnp.concatenate(lines, axis=0).T.astype(jnp.bfloat16)
    base = jnp.dot(lines, chosen, preferred_element_type=jnp.float32)
    for block in range(GROUP):
        for parity in range(PARITIES):
            shift = parity * SLOT + block * colors
            moved = pltpu.roll(base, shift, 1) if shift else base
            start = (block * PARITIES + parity) * channels
            first_out[start:start + channels, :] = moved.astype(jnp.bfloat16)

    none = jnp.zeros((channels, channels), jnp.bfloat16)
    for tap in range(TAPS * TAPS):
        taps = [second[tap * TAPS + tap_x] for tap_x in range(TAPS)]
        columns = slice(tap * VIEWS * channels, (tap + 1) * VIEWS * channels)
        second_out[:channels, columns] = jnp.concatenate(taps + [none], axis=1)
        second_out[channels:, columns] = jnp.concatenate([none] + taps, axis=1)

    out_rows = down_out.shape[0] // channels
    sum_rows = down_out.shape[1] // (TAPS * channels)
    taps = jnp.concatenate([down[tap] for tap in range(TAPS * TAPS)], axis=1)
    place = lax.broadcasted_iota(jnp.int32, (down_out.shape[0], channels), 0)
    channel = lax.broadcasted_iota(jnp.int32, (down_out.shape[0], channels), 1)
    total = None
    for y in range(out_rows):
        spread = (place == channel * out_rows + y).astype(jnp.float32).astype(jnp.bfloat16)
        pieces = [taps]
        before, after = 2 * y, sum_rows - TAPS - 2 * y
        if before:
            pieces = [jnp.zeros((channels, before * TAPS * channels), jnp.bfloat16)] + pieces
        if after:
            pieces = pieces + [jnp.zeros((channels, after * TAPS * channels), jnp.bfloat16)]
        part = jnp.dot(spread, jnp.concatenate(pieces, axis=1), preferred_element_type=jnp.float32)
        total = part if total is None else total + part
    down_out[...] = total.astype(jnp.bfloat16)


def encode_kernel(own_ref, there_ref, back_ref, gather_ref, columns_ref, live_ref, first_w, second_w, down_w, out_ref, lines, bands, act, held, taps, *, rows, frames):
    half = columns_ref.shape[1] // VIEWS
    channels = second_w.shape[0] // PARITIES
    pair = PARITIES * channels
    wide = (frames + 2) * half
    narrow = frames * half
    groups = -(-(rows + 3) // GROUP)
    odd = lax.rem(lax.axis_index("frames"), 2)
    row_device = lax.axis_index("rows")
    top, bottom = row_device == 0, row_device == lax.axis_size("rows") - 1
    keep_there = jnp.where(jnp.logical_or(jnp.logical_and(odd == 0, top), jnp.logical_and(odd == 1, bottom)), 0.0, 1.0)
    keep_back = jnp.where(jnp.logical_or(jnp.logical_and(odd == 1, top), jnp.logical_and(odd == 0, bottom)), 0.0, 1.0)
    size = own_ref.shape[0]
    lines[:size, :] = own_ref[...]
    lines[size:2 * size, :] = (there_ref[...].astype(jnp.float32) * keep_there).astype(jnp.bfloat16)
    lines[2 * size:, :] = (back_ref[...].astype(jnp.float32) * keep_back).astype(jnp.bfloat16)
    spread = jnp.dot(gather_ref[...], lines[...], preferred_element_type=jnp.float32).astype(jnp.bfloat16)
    spread = jnp.dot(spread, columns_ref[...], preferred_element_type=jnp.float32).astype(jnp.bfloat16)
    depth = VIEWS * SLOT
    for group in range(groups):
        for view in range(VIEWS):
            place = group * depth + view * SLOT
            for t in range(frames + 4):
                source = (t * groups + group) * SLOT
                bands[place:place + SLOT, t * half:(t + 1) * half] = spread[source:source + SLOT, view * half:(view + 1) * half]

    lane = lax.broadcasted_iota(jnp.int32, (channels, half), 1)
    for row in range(rows + 3):
        group, block = row // GROUP, row % GROUP
        band = jnp.concatenate([bands[group * depth:(group + 1) * depth, tap * half:tap * half + wide] for tap in range(TAPS)], axis=0)
        total = jnp.dot(first_w[block * pair:(block + 1) * pair, :], band, preferred_element_type=jnp.float32)
        first = (total * live_ref[row:row + 1, :]).astype(jnp.bfloat16)
        if 1 <= row <= rows + 1:
            held[(row - 1) * pair:row * pair, :] = first[:, 2 * half:]
        value = first.astype(jnp.float32)
        value = value / (1 + jnp.exp(-value))
        base = row * VIEWS * channels
        act[base + channels:base + 3 * channels, :] = value.astype(jnp.bfloat16)
        for t in range(frames + 2):
            lanes = slice(t * half, (t + 1) * half)
            left = jnp.where(lane == 0, 0.0, pltpu.roll(value[channels:, lanes], 1, 1))
            right = jnp.where(lane == half - 1, 0.0, pltpu.roll(value[:channels, lanes], half - 1, 1))
            act[base:base + channels, lanes] = left.astype(jnp.bfloat16)
            act[base + 3 * channels:base + 4 * channels, lanes] = right.astype(jnp.bfloat16)

    window = TAPS * VIEWS * channels
    for row in range(rows + 1):
        base = row * VIEWS * channels
        total = None
        for tap in range(TAPS):
            part = jnp.dot(
                second_w[:, tap * window:(tap + 1) * window],
                act[base:base + window, tap * half:tap * half + narrow],
                preferred_element_type=jnp.float32,
            )
            total = part if total is None else total + part
        second = total * live_ref[row + 1:row + 2, 2 * half:]
        value = (held[row * pair:(row + 1) * pair, :].astype(jnp.float32) + second).astype(jnp.bfloat16)
        base = row * TAPS * channels
        taps[base + channels:base + 3 * channels, :] = value
        value = value.astype(jnp.float32)
        for t in range(frames):
            lanes = slice(t * half, (t + 1) * half)
            left = jnp.where(lane == 0, 0.0, pltpu.roll(value[channels:, lanes], 1, 1))
            taps[base:base + channels, lanes] = left.astype(jnp.bfloat16)
    encoded = jnp.dot(down_w[...], taps[...], preferred_element_type=jnp.float32).astype(jnp.bfloat16)
    size = down_w.shape[0]
    for t in range(frames):
        out_ref[t * size:(t + 1) * size, :] = encoded[:, t * half:(t + 1) * half]


def hbm(array):
    return pltpu.with_memory_space_constraint(array, pltpu.HBM)


def snake(row_devices, frame_devices):
    route = []
    for left in range(0, frame_devices, 2):
        ring = [(row, left) for row in range(row_devices)] + [(row, left + 1) for row in reversed(range(row_devices))]
        ring = [row * frame_devices + frame for row, frame in ring]
        route += list(zip(ring, ring[1:] + ring[:1]))
    return route


def shards(pixels, frame_counts, weight_first, weight_second, weight_down):
    clips, frames, colors, rows, width = pixels.shape
    channels = weight_first.shape[3]
    half = width // 2
    out_rows = rows // 2
    frame_devices, row_devices = lax.axis_size("frames"), lax.axis_size("rows")
    assert clips == 1 and frames >= 4 and rows >= 3 and rows % 2 == 0
    assert (GROUP + 2) * colors <= SLOT and frame_devices % 2 == 0
    bf16 = jnp.bfloat16
    frame_device = lax.axis_index("frames")
    size = frames * colors * rows
    earlier = lax.ppermute(pixels[0, -4:], "frames", [(i, (i + 1) % frame_devices) for i in range(frame_devices)])
    late = lax.optimization_barrier(pixels[0].reshape(size, width))
    earlier = earlier.reshape(4 * colors * rows, width)
    earlier = jnp.where(frame_device > 0, earlier, jnp.zeros_like(earlier))
    own = jnp.concatenate([earlier, late], axis=0)
    own, weight_first = lax.optimization_barrier((own, weight_first))
    route = snake(row_devices, frame_devices)
    axes = ("rows", "frames")
    there = lax.ppermute(own, axes, route)
    back = lax.ppermute(own, axes, [(b, a) for a, b in route])

    pair = PARITIES * channels
    wide, narrow = (frames + 2) * half, frames * half
    depth = TAPS * VIEWS * SLOT
    groups = -(-(rows + 3) // GROUP)
    first_w, second_w, down_w, live, gather, columns = pl.pallas_call(
        lambda *refs: prepare_kernel(*refs, rows=rows, frames=frames),
        name="prepare",
        compiler_params=pltpu.CompilerParams(vmem_limit_bytes=8 << 20),
        in_specs=[SMEM] + [HBM] * 3,
        out_specs=[VMEM] * 6,
        out_shape=[
            jax.ShapeDtypeStruct((GROUP * pair, depth), bf16),
            jax.ShapeDtypeStruct((pair, TAPS * TAPS * VIEWS * channels), bf16),
            jax.ShapeDtypeStruct((channels * out_rows, (rows + 1) * TAPS * channels), bf16),
            jax.ShapeDtypeStruct((rows + 3, wide), jnp.float32),
            jax.ShapeDtypeStruct(((frames + 4) * groups * SLOT, 3 * own.shape[0]), bf16),
            jax.ShapeDtypeStruct((width, VIEWS * half), bf16),
        ],
        scratch_shapes=[
            pltpu.VMEM((TAPS**3, colors, channels), bf16),
            pltpu.VMEM((TAPS**3, channels, channels), bf16),
            pltpu.VMEM((TAPS**2, channels, channels), bf16),
            pltpu.SemaphoreType.DMA((3,)),
        ],
    )(
        frame_counts,
        hbm(weight_first.transpose(0, 1, 2, 4, 3).reshape(TAPS**3, colors, channels)),
        hbm(weight_second.reshape(TAPS**3, channels, channels)),
        hbm(weight_down.reshape(TAPS**2, channels, channels)),
    )
    encoded = pl.pallas_call(
        lambda *refs: encode_kernel(*refs, rows=rows, frames=frames),
        name="encode",
        compiler_params=pltpu.CompilerParams(vmem_limit_bytes=24 << 20),
        in_specs=[VMEM] * 9,
        out_specs=VMEM,
        out_shape=jax.ShapeDtypeStruct((frames * channels * out_rows, half), bf16),
        scratch_shapes=[
            pltpu.VMEM((3 * own.shape[0], width), bf16),
            pltpu.VMEM((groups * VIEWS * SLOT, (frames + 4) * half), bf16),
            pltpu.VMEM(((rows + 3) * VIEWS * channels, wide), bf16),
            pltpu.VMEM(((rows + 1) * pair, narrow), bf16),
            pltpu.VMEM(((rows + 1) * TAPS * channels, narrow), bf16),
        ],
    )(own, there, back, gather, columns, live, first_w, second_w, down_w)
    return encoded.reshape(1, frames, channels, out_rows, half)


def solution(mesh):
    in_specs = (
        P(("groups", "clips"), "frames", None, "rows", None),
        P(("groups", "clips")),
        P(),
        P(),
        P(),
    )
    out_specs = P(("groups", "clips"), "frames", None, "rows", None)
    return jax.shard_map(shards, mesh=mesh, in_specs=in_specs, out_specs=out_specs, check_vma=False)
```

```python
import jax
import jax.numpy as jnp
from jax import lax
from jax.experimental import pallas as pl
from jax.experimental.pallas import tpu as pltpu
from jax.sharding import PartitionSpec as P

VIEWS = 4
PARITIES = 2
TAPS = 3
GROUP = 3
SLOT = 16
SUBLANES = 8
HALVES = 2

VMEM = pl.BlockSpec(memory_space=pltpu.VMEM)
HBM = pl.BlockSpec(memory_space=pltpu.HBM)
SMEM = pl.BlockSpec(memory_space=pltpu.SMEM)


def one_hot(shape, target, valid):
    lane = lax.broadcasted_iota(jnp.int32, shape, 1)
    return jnp.where(lane == jnp.where(valid, target, -1), 1.0, 0.0).astype(jnp.bfloat16)


def prepare_kernel(count, first_hbm, second_hbm, down_hbm, first_out, second_out, down_out, live_out, gather_out, columns_out, first, second, down, sems, *, rows, frames):
    arrays = ((first_hbm, first), (second_hbm, second), (down_hbm, down))
    copies = [pltpu.make_async_copy(source, target, sems.at[i]) for i, (source, target) in enumerate(arrays)]
    for copy in copies:
        copy.start()
    channels = first.shape[2]
    colors = first.shape[1]

    size = TAPS**3 * SUBLANES
    line = lax.broadcasted_iota(jnp.int32, (size, 1), 0)
    tap, color = line // SUBLANES, line % SUBLANES
    target = (tap // TAPS**2 * VIEWS + tap % TAPS) * SLOT + tap // TAPS % TAPS * colors + color
    chosen = one_hot((size, first_out.shape[1]), target, color < colors)

    width = columns_out.shape[0]
    column = lax.broadcasted_iota(jnp.int32, columns_out.shape, 0)
    place = lax.broadcasted_iota(jnp.int32, columns_out.shape, 1)
    half = width // 2
    columns_out[...] = jnp.where(column == place % half * 2 + place // half - 1, 1.0, 0.0).astype(jnp.bfloat16)

    odd = lax.rem(lax.axis_index("frames"), 2)
    groups = -(-(rows + 3) // GROUP)
    line = lax.broadcasted_iota(jnp.int32, (gather_out.shape[0], 1), 0)
    frame, group, inner = line // (groups * SLOT), line // SLOT % groups, line % SLOT
    row, color = group * GROUP + inner // colors - 3, inner % colors
    source = jnp.where(row < 0, 1 + odd, jnp.where(row < rows, 0, 2 - odd))
    local = jnp.where(row < 0, row + rows, jnp.where(row < rows, row, row - rows))
    target = ((source * ((frames + 4) // HALVES) + frame) * colors + color) * rows + local
    gather_out[...] = one_hot(gather_out.shape, target, jnp.logical_and(inner < (GROUP + 2) * colors, row < rows + 2))

    half = live_out.shape[1] // (frames + 2)
    frame = lax.broadcasted_iota(jnp.int32, live_out.shape, 1) // half + (lax.axis_index("frames") * frames - 2)
    row = lax.broadcasted_iota(jnp.int32, live_out.shape, 0) + (lax.axis_index("rows") * rows - 2)
    inside = jnp.logical_and(row >= 0, row < lax.axis_size("rows") * rows)
    live_out[...] = jnp.where(jnp.logical_and(inside, frame < count[0]), 1.0, 0.0)

    for copy in copies:
        copy.wait()
    filler = jnp.zeros((SUBLANES - colors, channels), jnp.float32)
    lines = []
    for tap in range(TAPS**3):
        lines += [first[tap].astype(jnp.float32), filler]
    lines = jnp.concatenate(lines, axis=0).T.astype(jnp.bfloat16)
    base = jnp.dot(lines, chosen, preferred_element_type=jnp.float32)
    for block in range(GROUP):
        for parity in range(PARITIES):
            shift = parity * SLOT + block * colors
            moved = pltpu.roll(base, shift, 1) if shift else base
            start = (block * PARITIES + parity) * channels
            first_out[start:start + channels, :] = moved.astype(jnp.bfloat16)

    none = jnp.zeros((channels, channels), jnp.bfloat16)
    for tap in range(TAPS * TAPS):
        taps = [second[tap * TAPS + tap_x] for tap_x in range(TAPS)]
        columns = slice(tap * VIEWS * channels, (tap + 1) * VIEWS * channels)
        second_out[:channels, columns] = jnp.concatenate(taps + [none], axis=1)
        second_out[channels:, columns] = jnp.concatenate([none] + taps, axis=1)

    out_rows = down_out.shape[0] // channels
    sum_rows = down_out.shape[1] // (TAPS * channels)
    taps = jnp.concatenate([down[tap] for tap in range(TAPS * TAPS)], axis=1)
    place = lax.broadcasted_iota(jnp.int32, (down_out.shape[0], channels), 0)
    channel = lax.broadcasted_iota(jnp.int32, (down_out.shape[0], channels), 1)
    total = None
    for y in range(out_rows):
        spread = (place == channel * out_rows + y).astype(jnp.float32).astype(jnp.bfloat16)
        pieces = [taps]
        before, after = 2 * y, sum_rows - TAPS - 2 * y
        if before:
            pieces = [jnp.zeros((channels, before * TAPS * channels), jnp.bfloat16)] + pieces
        if after:
            pieces = pieces + [jnp.zeros((channels, after * TAPS * channels), jnp.bfloat16)]
        part = jnp.dot(spread, jnp.concatenate(pieces, axis=1), preferred_element_type=jnp.float32)
        total = part if total is None else total + part
    down_out[...] = total.astype(jnp.bfloat16)


def encode_kernel(own_ref, there_ref, back_ref, gather_ref, columns_ref, live_ref, first_w, second_w, down_w, out_ref, lines, bands, act, held, taps, *, rows, frames):
    half = columns_ref.shape[1] // VIEWS
    channels = second_w.shape[0] // PARITIES
    pair = PARITIES * channels
    wide = (frames + 2) * half
    narrow = frames * half
    groups = -(-(rows + 3) // GROUP)
    odd = lax.rem(lax.axis_index("frames"), 2)
    row_device = lax.axis_index("rows")
    top, bottom = row_device == 0, row_device == lax.axis_size("rows") - 1
    keep_there = jnp.where(jnp.logical_or(jnp.logical_and(odd == 0, top), jnp.logical_and(odd == 1, bottom)), 0.0, 1.0).astype(jnp.bfloat16)
    keep_back = jnp.where(jnp.logical_or(jnp.logical_and(odd == 1, top), jnp.logical_and(odd == 0, bottom)), 0.0, 1.0).astype(jnp.bfloat16)
    size = own_ref.shape[0] // HALVES
    count = (frames + 4) // HALVES
    depth = VIEWS * SLOT
    for part in range(HALVES):
        rows_of = slice(part * size, (part + 1) * size)
        base = part * 3 * size
        lines[base:base + size, :] = own_ref[rows_of, :]
        lines[base + size:base + 2 * size, :] = there_ref[rows_of, :] * keep_there
        lines[base + 2 * size:base + 3 * size, :] = back_ref[rows_of, :] * keep_back
        spread = jnp.dot(gather_ref[...], lines[base:base + 3 * size, :], preferred_element_type=jnp.float32).astype(jnp.bfloat16)
        spread = jnp.dot(spread, columns_ref[...], preferred_element_type=jnp.float32).astype(jnp.bfloat16)
        for t in range(count):
            lanes = slice((part * count + t) * half, (part * count + t + 1) * half)
            for group in range(groups):
                source = (t * groups + group) * SLOT
                for view in range(VIEWS):
                    place = group * depth + view * SLOT
                    bands[place:place + SLOT, lanes] = spread[source:source + SLOT, view * half:(view + 1) * half]

    lane = lax.broadcasted_iota(jnp.int32, (channels, half), 1)
    zero = jnp.zeros((channels, half), jnp.bfloat16)

    def to_right(value):
        return jnp.where(lane == 0, zero, pltpu.roll(value, 1, 1))

    def to_left(value):
        return jnp.where(lane == half - 1, zero, pltpu.roll(value, half - 1, 1))

    step = 2 * half

    def first_conv(group, chunk):
        lanes = slice(chunk * step, (chunk + 1) * step)
        blocks = min(GROUP, rows + 3 - group * GROUP)
        band = [bands[group * depth:(group + 1) * depth, tap * half + chunk * step:tap * half + (chunk + 1) * step] for tap in range(TAPS)]
        total = jnp.dot(first_w[:blocks * pair, :], jnp.concatenate(band, axis=0), preferred_element_type=jnp.float32)
        for block in range(blocks):
            row = group * GROUP + block
            first = total[block * pair:(block + 1) * pair, :].astype(jnp.bfloat16) * live_ref[row:row + 1, lanes].astype(jnp.bfloat16)
            if 1 <= row <= rows + 1 and chunk > 0:
                held[(row - 1) * pair:row * pair, (chunk - 1) * step:chunk * step] = first
            value = 0.5 * first.astype(jnp.float32)
            value = (value + value * jnp.tanh(value)).astype(jnp.bfloat16)
            base = row * VIEWS * channels
            act[base + channels:base + 3 * channels, lanes] = value
            for t in range(2):
                inner = slice(t * half, (t + 1) * half)
                outer = slice(chunk * step + t * half, chunk * step + (t + 1) * half)
                act[base:base + channels, outer] = to_right(value[channels:, inner])
                act[base + 3 * channels:base + 4 * channels, outer] = to_left(value[:channels, inner])

    window = TAPS * VIEWS * channels

    def second_conv(row, chunk):
        base = row * VIEWS * channels
        source = [act[base:base + window, tap * half + chunk * step:tap * half + (chunk + 1) * step] for tap in range(TAPS)]
        total = jnp.dot(second_w[...], jnp.concatenate(source, axis=0), preferred_element_type=jnp.float32)
        second = total * live_ref[row + 1:row + 2, (chunk + 1) * step:(chunk + 2) * step]
        lanes = slice(chunk * step, (chunk + 1) * step)
        value = (held[row * pair:(row + 1) * pair, lanes].astype(jnp.float32) + second).astype(jnp.bfloat16)
        base = row * TAPS * channels
        taps[base + channels:base + 3 * channels, lanes] = value
        for t in range(2):
            outer = slice(chunk * step + t * half, chunk * step + (t + 1) * half)
            taps[base:base + channels, outer] = to_right(value[channels:, t * half:(t + 1) * half])

    def down_conv(chunk, first_row, last_row):
        lanes = slice(chunk * step, (chunk + 1) * step)
        depths = slice(first_row * TAPS * channels, last_row * TAPS * channels)
        return jnp.dot(down_w[:, depths], taps[depths, lanes], preferred_element_type=jnp.float32)

    chunks = frames // 2
    waiting = []
    for group in range(groups):
        for chunk in range(chunks + 1):
            first_conv(group, chunk)
            if chunk == chunks:
                waiting += [row for row in range(rows + 1) if group * GROUP <= row + 2 < (group + 1) * GROUP]
            if chunk in (0, chunks) and waiting and waiting[0] < rows:
                row = waiting.pop(0)
                for part in range(chunks):
                    second_conv(row, part)
    for row in waiting[:-1]:
        for part in range(chunks):
            second_conv(row, part)
    early = [down_conv(part, 0, rows) for part in range(chunks)]
    for part in range(chunks):
        second_conv(rows, part)
    size = down_w.shape[0]
    for part in range(chunks):
        encoded = (early[part] + down_conv(part, rows, rows + 1)).astype(jnp.bfloat16)
        for t in range(2):
            frame = part * 2 + t
            out_ref[frame * size:(frame + 1) * size, :] = encoded[:, t * half:(t + 1) * half]


def hbm(array):
    return pltpu.with_memory_space_constraint(array, pltpu.HBM)


def snake(row_devices, frame_devices):
    route = []
    for left in range(0, frame_devices, 2):
        ring = [(row, left) for row in range(row_devices)] + [(row, left + 1) for row in reversed(range(row_devices))]
        ring = [row * frame_devices + frame for row, frame in ring]
        route += list(zip(ring, ring[1:] + ring[:1]))
    return route


def shards(pixels, frame_counts, weight_first, weight_second, weight_down):
    clips, frames, colors, rows, width = pixels.shape
    channels = weight_first.shape[3]
    half = width // 2
    out_rows = rows // 2
    frame_devices, row_devices = lax.axis_size("frames"), lax.axis_size("rows")
    assert clips == 1 and frames >= 4 and rows >= 3 and rows % 2 == 0
    assert (GROUP + 2) * colors <= SLOT and frame_devices % 2 == 0
    bf16 = jnp.bfloat16
    frame_device = lax.axis_index("frames")
    size = frames * colors * rows
    earlier = lax.ppermute(pixels[0, -4:], "frames", [(i, (i + 1) % frame_devices) for i in range(frame_devices)])
    late = lax.optimization_barrier(pixels[0].reshape(size, width))
    earlier = earlier.reshape(4 * colors * rows, width)
    earlier = jnp.where(frame_device > 0, earlier, jnp.zeros_like(earlier))
    own = jnp.concatenate([earlier, late], axis=0)
    own, weight_first, frame_counts = lax.optimization_barrier((own, weight_first, frame_counts))
    route = snake(row_devices, frame_devices)
    axes = ("rows", "frames")
    there = lax.ppermute(own, axes, route)
    back = lax.ppermute(own, axes, [(b, a) for a, b in route])

    pair = PARITIES * channels
    wide, narrow = (frames + 2) * half, frames * half
    depth = TAPS * VIEWS * SLOT
    groups = -(-(rows + 3) // GROUP)
    first_w, second_w, down_w, live, gather, columns = pl.pallas_call(
        lambda *refs: prepare_kernel(*refs, rows=rows, frames=frames),
        name="prepare",
        compiler_params=pltpu.CompilerParams(vmem_limit_bytes=8 << 20),
        in_specs=[SMEM] + [HBM] * 3,
        out_specs=[VMEM] * 6,
        out_shape=[
            jax.ShapeDtypeStruct((GROUP * pair, depth), bf16),
            jax.ShapeDtypeStruct((pair, TAPS * TAPS * VIEWS * channels), bf16),
            jax.ShapeDtypeStruct((channels * out_rows, (rows + 1) * TAPS * channels), bf16),
            jax.ShapeDtypeStruct((rows + 3, wide), jnp.float32),
            jax.ShapeDtypeStruct(((frames + 4) // HALVES * groups * SLOT, 3 * own.shape[0] // HALVES), bf16),
            jax.ShapeDtypeStruct((width, VIEWS * half), bf16),
        ],
        scratch_shapes=[
            pltpu.VMEM((TAPS**3, colors, channels), bf16),
            pltpu.VMEM((TAPS**3, channels, channels), bf16),
            pltpu.VMEM((TAPS**2, channels, channels), bf16),
            pltpu.SemaphoreType.DMA((3,)),
        ],
    )(
        frame_counts,
        hbm(weight_first.transpose(0, 1, 2, 4, 3).reshape(TAPS**3, colors, channels)),
        hbm(weight_second.reshape(TAPS**3, channels, channels)),
        hbm(weight_down.reshape(TAPS**2, channels, channels)),
    )
    encoded = pl.pallas_call(
        lambda *refs: encode_kernel(*refs, rows=rows, frames=frames),
        name="encode",
        compiler_params=pltpu.CompilerParams(vmem_limit_bytes=24 << 20),
        in_specs=[VMEM] * 9,
        out_specs=VMEM,
        out_shape=jax.ShapeDtypeStruct((frames * channels * out_rows, half), bf16),
        scratch_shapes=[
            pltpu.VMEM((3 * own.shape[0], width), bf16),
            pltpu.VMEM((groups * VIEWS * SLOT, (frames + 4) * half), bf16),
            pltpu.VMEM(((rows + 3) * VIEWS * channels, wide), bf16),
            pltpu.VMEM(((rows + 1) * pair, narrow), bf16),
            pltpu.VMEM(((rows + 1) * TAPS * channels, narrow), bf16),
        ],
    )(own, there, back, gather, columns, live, first_w, second_w, down_w)
    return encoded.reshape(1, frames, channels, out_rows, half)


def solution(mesh):
    in_specs = (
        P(("groups", "clips"), "frames", None, "rows", None),
        P(("groups", "clips")),
        P(),
        P(),
        P(),
    )
    out_specs = P(("groups", "clips"), "frames", None, "rows", None)
    return jax.shard_map(shards, mesh=mesh, in_specs=in_specs, out_specs=out_specs, check_vma=False)
```

```python
import jax
import jax.numpy as jnp
from jax import lax
from jax.experimental import pallas as pl
from jax.experimental.pallas import tpu as pltpu
from jax.sharding import PartitionSpec as P

VIEWS = 4
PARITIES = 2
TAPS = 3
GROUP = 3
SLOT = 16
SUBLANES = 8
HALVES = 2

VMEM = pl.BlockSpec(memory_space=pltpu.VMEM)
HBM = pl.BlockSpec(memory_space=pltpu.HBM)
SMEM = pl.BlockSpec(memory_space=pltpu.SMEM)


def one_hot(shape, target, valid):
    lane = lax.broadcasted_iota(jnp.int32, shape, 1)
    return jnp.where(lane == jnp.where(valid, target, -1), 1.0, 0.0).astype(jnp.bfloat16)


def prepare_kernel(count, first_hbm, second_hbm, down_hbm, first_out, second_out, down_out, live_out, gather_out, columns_out, first, second, down, sems, *, rows, frames):
    arrays = ((first_hbm, first), (second_hbm, second), (down_hbm, down))
    copies = [pltpu.make_async_copy(source, target, sems.at[i]) for i, (source, target) in enumerate(arrays)]
    for copy in copies:
        copy.start()
    channels = first.shape[2]
    colors = first.shape[1]

    size = TAPS**3 * SUBLANES
    line = lax.broadcasted_iota(jnp.int32, (size, 1), 0)
    tap, color = line // SUBLANES, line % SUBLANES
    target = (tap // TAPS**2 * VIEWS + tap % TAPS) * SLOT + tap // TAPS % TAPS * colors + color
    chosen = one_hot((size, first_out.shape[1]), target, color < colors)

    width = columns_out.shape[0]
    column = lax.broadcasted_iota(jnp.int32, columns_out.shape, 0)
    place = lax.broadcasted_iota(jnp.int32, columns_out.shape, 1)
    half = width // 2
    columns_out[...] = jnp.where(column == place % half * 2 + place // half - 1, 1.0, 0.0).astype(jnp.bfloat16)

    odd = lax.rem(lax.axis_index("frames"), 2)
    groups = -(-(rows + 3) // GROUP)
    line = lax.broadcasted_iota(jnp.int32, (gather_out.shape[0], 1), 0)
    frame, group, inner = line // (groups * SLOT), line // SLOT % groups, line % SLOT
    row, color = group * GROUP + inner // colors - 3, inner % colors
    source = jnp.where(row < 0, 1 + odd, jnp.where(row < rows, 0, 2 - odd))
    local = jnp.where(row < 0, row + rows, jnp.where(row < rows, row, row - rows))
    target = ((source * ((frames + 4) // HALVES) + frame) * colors + color) * rows + local
    gather_out[...] = one_hot(gather_out.shape, target, jnp.logical_and(inner < (GROUP + 2) * colors, row < rows + 2))

    half = live_out.shape[1] // (frames + 2)
    frame = lax.broadcasted_iota(jnp.int32, live_out.shape, 1) // half + (lax.axis_index("frames") * frames - 2)
    row = lax.broadcasted_iota(jnp.int32, live_out.shape, 0) + (lax.axis_index("rows") * rows - 2)
    inside = jnp.logical_and(row >= 0, row < lax.axis_size("rows") * rows)
    live_out[...] = jnp.where(jnp.logical_and(inside, frame < count[0]), 1.0, 0.0)

    for copy in copies:
        copy.wait()
    filler = jnp.zeros((SUBLANES - colors, channels), jnp.float32)
    lines = []
    for tap in range(TAPS**3):
        lines += [first[tap].astype(jnp.float32), filler]
    lines = jnp.concatenate(lines, axis=0).T.astype(jnp.bfloat16)
    base = jnp.dot(lines, chosen, preferred_element_type=jnp.float32)
    for block in range(GROUP):
        for parity in range(PARITIES):
            shift = parity * SLOT + block * colors
            moved = pltpu.roll(base, shift, 1) if shift else base
            start = (block * PARITIES + parity) * channels
            first_out[start:start + channels, :] = moved.astype(jnp.bfloat16)

    none = jnp.zeros((channels, channels), jnp.bfloat16)
    for tap in range(TAPS * TAPS):
        taps = [second[tap * TAPS + tap_x] for tap_x in range(TAPS)]
        columns = slice(tap * VIEWS * channels, (tap + 1) * VIEWS * channels)
        second_out[:channels, columns] = jnp.concatenate(taps + [none], axis=1)
        second_out[channels:, columns] = jnp.concatenate([none] + taps, axis=1)

    out_rows = down_out.shape[0] // channels
    sum_rows = down_out.shape[1] // (TAPS * channels)
    taps = jnp.concatenate([down[tap] for tap in range(TAPS * TAPS)], axis=1)
    place = lax.broadcasted_iota(jnp.int32, (down_out.shape[0], channels), 0)
    channel = lax.broadcasted_iota(jnp.int32, (down_out.shape[0], channels), 1)
    total = None
    for y in range(out_rows):
        spread = (place == channel * out_rows + y).astype(jnp.float32).astype(jnp.bfloat16)
        pieces = [taps]
        before, after = 2 * y, sum_rows - TAPS - 2 * y
        if before:
            pieces = [jnp.zeros((channels, before * TAPS * channels), jnp.bfloat16)] + pieces
        if after:
            pieces = pieces + [jnp.zeros((channels, after * TAPS * channels), jnp.bfloat16)]
        part = jnp.dot(spread, jnp.concatenate(pieces, axis=1), preferred_element_type=jnp.float32)
        total = part if total is None else total + part
    down_out[...] = total.astype(jnp.bfloat16)


def encode_kernel(own_ref, there_ref, back_ref, gather_ref, columns_ref, live_ref, first_w, second_w, down_w, out_ref, lines, bands, act, held, taps, *, rows, frames):
    half = columns_ref.shape[1] // VIEWS
    channels = second_w.shape[0] // PARITIES
    pair = PARITIES * channels
    wide = (frames + 2) * half
    narrow = frames * half
    groups = -(-(rows + 3) // GROUP)
    odd = lax.rem(lax.axis_index("frames"), 2)
    row_device = lax.axis_index("rows")
    top, bottom = row_device == 0, row_device == lax.axis_size("rows") - 1
    keep_there = jnp.where(jnp.logical_or(jnp.logical_and(odd == 0, top), jnp.logical_and(odd == 1, bottom)), 0.0, 1.0).astype(jnp.bfloat16)
    keep_back = jnp.where(jnp.logical_or(jnp.logical_and(odd == 1, top), jnp.logical_and(odd == 0, bottom)), 0.0, 1.0).astype(jnp.bfloat16)
    size = own_ref.shape[0] // HALVES
    count = (frames + 4) // HALVES
    depth = VIEWS * SLOT
    for part in range(HALVES):
        rows_of = slice(part * size, (part + 1) * size)
        base = part * 3 * size
        lines[base:base + size, :] = own_ref[rows_of, :]
        lines[base + size:base + 2 * size, :] = there_ref[rows_of, :] * keep_there
        lines[base + 2 * size:base + 3 * size, :] = back_ref[rows_of, :] * keep_back
        spread = jnp.dot(gather_ref[...], lines[base:base + 3 * size, :], preferred_element_type=jnp.float32).astype(jnp.bfloat16)
        spread = jnp.dot(spread, columns_ref[...], preferred_element_type=jnp.float32).astype(jnp.bfloat16)
        for t in range(count):
            lanes = slice((part * count + t) * half, (part * count + t + 1) * half)
            for group in range(groups):
                source = (t * groups + group) * SLOT
                for view in range(VIEWS):
                    place = group * depth + view * SLOT
                    bands[place:place + SLOT, lanes] = spread[source:source + SLOT, view * half:(view + 1) * half]

    lane = lax.broadcasted_iota(jnp.int32, (channels, half), 1)
    zero = jnp.zeros((channels, half), jnp.bfloat16)

    def to_right(value):
        return jnp.where(lane == 0, zero, pltpu.roll(value, 1, 1))

    def to_left(value):
        return jnp.where(lane == half - 1, zero, pltpu.roll(value, half - 1, 1))

    step = 2 * half

    def first_dot(group, chunk):
        blocks = min(GROUP, rows + 3 - group * GROUP)
        band = [bands[group * depth:(group + 1) * depth, tap * half + chunk * step:tap * half + (chunk + 1) * step] for tap in range(TAPS)]
        return jnp.dot(first_w[:blocks * pair, :], jnp.concatenate(band, axis=0), preferred_element_type=jnp.float32)

    def first_rest(group, chunk, total):
        lanes = slice(chunk * step, (chunk + 1) * step)
        for block in range(total.shape[0] // pair):
            row = group * GROUP + block
            first = total[block * pair:(block + 1) * pair, :].astype(jnp.bfloat16) * live_ref[row:row + 1, lanes].astype(jnp.bfloat16)
            if 1 <= row <= rows + 1 and chunk > 0:
                held[(row - 1) * pair:row * pair, (chunk - 1) * step:chunk * step] = first
            value = 0.5 * first.astype(jnp.float32)
            value = (value + value * jnp.tanh(value)).astype(jnp.bfloat16)
            base = row * VIEWS * channels
            act[base + channels:base + 3 * channels, lanes] = value
            for t in range(2):
                inner = slice(t * half, (t + 1) * half)
                outer = slice(chunk * step + t * half, chunk * step + (t + 1) * half)
                act[base:base + channels, outer] = to_right(value[channels:, inner])
                act[base + 3 * channels:base + 4 * channels, outer] = to_left(value[:channels, inner])

    def second_dot(row, chunk):
        window = TAPS * VIEWS * channels
        base = row * VIEWS * channels
        source = [act[base:base + window, tap * half + chunk * step:tap * half + (chunk + 1) * step] for tap in range(TAPS)]
        return jnp.dot(second_w[...], jnp.concatenate(source, axis=0), preferred_element_type=jnp.float32)

    def second_rest(row, chunk, parts):
        second = parts * live_ref[row + 1:row + 2, (chunk + 1) * step:(chunk + 2) * step]
        lanes = slice(chunk * step, (chunk + 1) * step)
        value = (held[row * pair:(row + 1) * pair, lanes].astype(jnp.float32) + second).astype(jnp.bfloat16)
        base = row * TAPS * channels
        taps[base + channels:base + 3 * channels, lanes] = value
        for t in range(2):
            outer = slice(chunk * step + t * half, chunk * step + (t + 1) * half)
            taps[base:base + channels, outer] = to_right(value[channels:, t * half:(t + 1) * half])

    def down_conv(chunk, first_row, last_row):
        lanes = slice(chunk * step, (chunk + 1) * step)
        depths = slice(first_row * TAPS * channels, last_row * TAPS * channels)
        return jnp.dot(down_w[:, depths], taps[depths, lanes], preferred_element_type=jnp.float32)

    chunks = frames // 2
    pieces = [(group, chunk) for group in range(groups) for chunk in range(chunks + 1)]
    waiting, final = [], [(rows, part) for part in range(chunks)]
    total = first_dot(*pieces[0])
    for number, (group, chunk) in enumerate(pieces):
        beside = waiting.pop(0) if waiting else None
        parts = second_dot(*beside) if beside else None
        later = first_dot(*pieces[number + 1]) if number + 1 < len(pieces) else None
        first_rest(group, chunk, total)
        if beside:
            second_rest(*beside, parts)
        total = later
        if chunk > 0:
            for row in range(rows):
                if group == (row + 2) // GROUP:
                    waiting.append((row, chunk - 1))
    for row, part in waiting:
        second_rest(row, part, second_dot(row, part))
    early = [down_conv(part, 0, rows) for part in range(chunks)]
    parts = [second_dot(*piece) for piece in final]
    for piece, part in zip(final, parts):
        second_rest(*piece, part)
    size = down_w.shape[0]
    for part in range(chunks):
        encoded = (early[part] + down_conv(part, rows, rows + 1)).astype(jnp.bfloat16)
        for t in range(2):
            frame = part * 2 + t
            out_ref[frame * size:(frame + 1) * size, :] = encoded[:, t * half:(t + 1) * half]


def hbm(array):
    return pltpu.with_memory_space_constraint(array, pltpu.HBM)


def snake(row_devices, frame_devices):
    route = []
    for left in range(0, frame_devices, 2):
        ring = [(row, left) for row in range(row_devices)] + [(row, left + 1) for row in reversed(range(row_devices))]
        ring = [row * frame_devices + frame for row, frame in ring]
        route += list(zip(ring, ring[1:] + ring[:1]))
    return route


def shards(pixels, frame_counts, weight_first, weight_second, weight_down):
    clips, frames, colors, rows, width = pixels.shape
    channels = weight_first.shape[3]
    half = width // 2
    out_rows = rows // 2
    frame_devices, row_devices = lax.axis_size("frames"), lax.axis_size("rows")
    assert clips == 1 and frames >= 4 and rows >= 3 and rows % 2 == 0
    assert (GROUP + 2) * colors <= SLOT and frame_devices % 2 == 0
    bf16 = jnp.bfloat16
    frame_device = lax.axis_index("frames")
    size = frames * colors * rows
    earlier = lax.ppermute(pixels[0, -4:], "frames", [(i, (i + 1) % frame_devices) for i in range(frame_devices)])
    late = lax.optimization_barrier(pixels[0].reshape(size, width))
    earlier = earlier.reshape(4 * colors * rows, width)
    earlier = jnp.where(frame_device > 0, earlier, jnp.zeros_like(earlier))
    own = jnp.concatenate([earlier, late], axis=0)
    own, weight_first, frame_counts = lax.optimization_barrier((own, weight_first, frame_counts))
    route = snake(row_devices, frame_devices)
    axes = ("rows", "frames")
    there = lax.ppermute(own, axes, route)
    back = lax.ppermute(own, axes, [(b, a) for a, b in route])

    pair = PARITIES * channels
    wide, narrow = (frames + 2) * half, frames * half
    depth = TAPS * VIEWS * SLOT
    groups = -(-(rows + 3) // GROUP)
    first_w, second_w, down_w, live, gather, columns = pl.pallas_call(
        lambda *refs: prepare_kernel(*refs, rows=rows, frames=frames),
        name="prepare",
        compiler_params=pltpu.CompilerParams(vmem_limit_bytes=8 << 20),
        in_specs=[SMEM] + [HBM] * 3,
        out_specs=[VMEM] * 6,
        out_shape=[
            jax.ShapeDtypeStruct((GROUP * pair, depth), bf16),
            jax.ShapeDtypeStruct((pair, TAPS * TAPS * VIEWS * channels), bf16),
            jax.ShapeDtypeStruct((channels * out_rows, (rows + 1) * TAPS * channels), bf16),
            jax.ShapeDtypeStruct((rows + 3, wide), jnp.float32),
            jax.ShapeDtypeStruct(((frames + 4) // HALVES * groups * SLOT, 3 * own.shape[0] // HALVES), bf16),
            jax.ShapeDtypeStruct((width, VIEWS * half), bf16),
        ],
        scratch_shapes=[
            pltpu.VMEM((TAPS**3, colors, channels), bf16),
            pltpu.VMEM((TAPS**3, channels, channels), bf16),
            pltpu.VMEM((TAPS**2, channels, channels), bf16),
            pltpu.SemaphoreType.DMA((3,)),
        ],
    )(
        frame_counts,
        hbm(weight_first.transpose(0, 1, 2, 4, 3).reshape(TAPS**3, colors, channels)),
        hbm(weight_second.reshape(TAPS**3, channels, channels)),
        hbm(weight_down.reshape(TAPS**2, channels, channels)),
    )
    encoded = pl.pallas_call(
        lambda *refs: encode_kernel(*refs, rows=rows, frames=frames),
        name="encode",
        compiler_params=pltpu.CompilerParams(vmem_limit_bytes=24 << 20),
        in_specs=[VMEM] * 9,
        out_specs=VMEM,
        out_shape=jax.ShapeDtypeStruct((frames * channels * out_rows, half), bf16),
        scratch_shapes=[
            pltpu.VMEM((3 * own.shape[0], width), bf16),
            pltpu.VMEM((groups * VIEWS * SLOT, (frames + 4) * half), bf16),
            pltpu.VMEM(((rows + 3) * VIEWS * channels, wide), bf16),
            pltpu.VMEM(((rows + 1) * pair, narrow), bf16),
            pltpu.VMEM(((rows + 1) * TAPS * channels, narrow), bf16),
        ],
    )(own, there, back, gather, columns, live, first_w, second_w, down_w)
    return encoded.reshape(1, frames, channels, out_rows, half)


def solution(mesh):
    in_specs = (
        P(("groups", "clips"), "frames", None, "rows", None),
        P(("groups", "clips")),
        P(),
        P(),
        P(),
    )
    out_specs = P(("groups", "clips"), "frames", None, "rows", None)
    return jax.shard_map(shards, mesh=mesh, in_specs=in_specs, out_specs=out_specs, check_vma=False)
```

```python
import jax
import jax.numpy as jnp
from jax import lax
from jax.experimental import pallas as pl
from jax.experimental.pallas import tpu as pltpu
from jax.sharding import PartitionSpec as P

VIEWS = 4
PARITIES = 2
TAPS = 3
GROUP = 3
SLOT = 16
SUBLANES = 8
HALVES = 2

VMEM = pl.BlockSpec(memory_space=pltpu.VMEM)
HBM = pl.BlockSpec(memory_space=pltpu.HBM)
SMEM = pl.BlockSpec(memory_space=pltpu.SMEM)


def one_hot(shape, target, valid):
    lane = lax.broadcasted_iota(jnp.int32, shape, 1)
    return jnp.where(lane == jnp.where(valid, target, -1), 1.0, 0.0).astype(jnp.bfloat16)


def prepare_kernel(count, first_hbm, second_hbm, down_hbm, first_out, second_out, down_out, live_out, gather_out, columns_out, first, second, down, sems, *, rows, frames):
    arrays = ((first_hbm, first), (second_hbm, second), (down_hbm, down))
    copies = [pltpu.make_async_copy(source, target, sems.at[i]) for i, (source, target) in enumerate(arrays)]
    for copy in copies:
        copy.start()
    channels = first.shape[2]
    colors = first.shape[1]

    size = TAPS**3 * SUBLANES
    line = lax.broadcasted_iota(jnp.int32, (size, 1), 0)
    tap, color = line // SUBLANES, line % SUBLANES
    target = (tap // TAPS**2 * VIEWS + tap % TAPS) * SLOT + tap // TAPS % TAPS * colors + color
    chosen = one_hot((size, first_out.shape[1]), target, color < colors)

    width = columns_out.shape[0]
    column = lax.broadcasted_iota(jnp.int32, columns_out.shape, 0)
    place = lax.broadcasted_iota(jnp.int32, columns_out.shape, 1)
    half = width // 2
    columns_out[...] = jnp.where(column == place % half * 2 + place // half - 1, 1.0, 0.0).astype(jnp.bfloat16)

    odd = lax.rem(lax.axis_index("frames"), 2)
    groups = -(-(rows + 3) // GROUP)
    line = lax.broadcasted_iota(jnp.int32, (gather_out.shape[0], 1), 0)
    frame, group, inner = line // (groups * SLOT), line // SLOT % groups, line % SLOT
    row, color = group * GROUP + inner // colors - 3, inner % colors
    source = jnp.where(row < 0, 1 + odd, jnp.where(row < rows, 0, 2 - odd))
    local = jnp.where(row < 0, row + rows, jnp.where(row < rows, row, row - rows))
    target = ((source * ((frames + 4) // HALVES) + frame) * colors + color) * rows + local
    gather_out[...] = one_hot(gather_out.shape, target, jnp.logical_and(inner < (GROUP + 2) * colors, row < rows + 2))

    half = live_out.shape[1] // (frames + 2)
    frame = lax.broadcasted_iota(jnp.int32, live_out.shape, 1) // half + (lax.axis_index("frames") * frames - 2)
    row = lax.broadcasted_iota(jnp.int32, live_out.shape, 0) + (lax.axis_index("rows") * rows - 2)
    inside = jnp.logical_and(row >= 0, row < lax.axis_size("rows") * rows)
    live_out[...] = jnp.where(jnp.logical_and(inside, frame < count[0]), 1.0, 0.0)

    for copy in copies:
        copy.wait()
    filler = jnp.zeros((SUBLANES - colors, channels), jnp.float32)
    lines = []
    for tap in range(TAPS**3):
        lines += [first[tap].astype(jnp.float32), filler]
    lines = jnp.concatenate(lines, axis=0).T.astype(jnp.bfloat16)
    base = jnp.dot(lines, chosen, preferred_element_type=jnp.float32)
    for block in range(GROUP):
        for parity in range(PARITIES):
            shift = parity * SLOT + block * colors
            moved = pltpu.roll(base, shift, 1) if shift else base
            start = (block * PARITIES + parity) * channels
            first_out[start:start + channels, :] = moved.astype(jnp.bfloat16)

    none = jnp.zeros((channels, channels), jnp.bfloat16)
    for tap in range(TAPS * TAPS):
        taps = [second[tap * TAPS + tap_x] for tap_x in range(TAPS)]
        columns = slice(tap * VIEWS * channels, (tap + 1) * VIEWS * channels)
        second_out[:channels, columns] = jnp.concatenate(taps + [none], axis=1)
        second_out[channels:, columns] = jnp.concatenate([none] + taps, axis=1)

    out_rows = down_out.shape[0] // channels
    sum_rows = down_out.shape[1] // (TAPS * channels)
    taps = jnp.concatenate([down[tap] for tap in range(TAPS * TAPS)], axis=1)
    place = lax.broadcasted_iota(jnp.int32, (down_out.shape[0], channels), 0)
    channel = lax.broadcasted_iota(jnp.int32, (down_out.shape[0], channels), 1)
    total = None
    for y in range(out_rows):
        spread = (place == channel * out_rows + y).astype(jnp.float32).astype(jnp.bfloat16)
        pieces = [taps]
        before, after = 2 * y, sum_rows - TAPS - 2 * y
        if before:
            pieces = [jnp.zeros((channels, before * TAPS * channels), jnp.bfloat16)] + pieces
        if after:
            pieces = pieces + [jnp.zeros((channels, after * TAPS * channels), jnp.bfloat16)]
        part = jnp.dot(spread, jnp.concatenate(pieces, axis=1), preferred_element_type=jnp.float32)
        total = part if total is None else total + part
    down_out[...] = total.astype(jnp.bfloat16)


def encode_kernel(own_ref, there_ref, back_ref, gather_ref, columns_ref, live_ref, first_w, second_w, down_w, out_ref, lines, bands, act, held, taps, *, rows, frames):
    half = columns_ref.shape[1] // VIEWS
    channels = second_w.shape[0] // PARITIES
    pair = PARITIES * channels
    groups = -(-(rows + 3) // GROUP)
    odd = lax.rem(lax.axis_index("frames"), 2)
    row_device = lax.axis_index("rows")
    top, bottom = row_device == 0, row_device == lax.axis_size("rows") - 1
    keep_there = jnp.where(jnp.logical_or(jnp.logical_and(odd == 0, top), jnp.logical_and(odd == 1, bottom)), 0.0, 1.0).astype(jnp.bfloat16)
    keep_back = jnp.where(jnp.logical_or(jnp.logical_and(odd == 1, top), jnp.logical_and(odd == 0, bottom)), 0.0, 1.0).astype(jnp.bfloat16)
    size = own_ref.shape[0] // HALVES
    count = (frames + 4) // HALVES
    depth = VIEWS * SLOT
    for part in range(HALVES):
        rows_of = slice(part * size, (part + 1) * size)
        base = part * 3 * size
        lines[base:base + size, :] = own_ref[rows_of, :]
        lines[base + size:base + 2 * size, :] = there_ref[rows_of, :] * keep_there
        lines[base + 2 * size:base + 3 * size, :] = back_ref[rows_of, :] * keep_back
        spread = jnp.dot(gather_ref[...], lines[base:base + 3 * size, :], preferred_element_type=jnp.float32).astype(jnp.bfloat16)
        spread = jnp.dot(spread, columns_ref[...], preferred_element_type=jnp.float32).astype(jnp.bfloat16)
        for t in range(count):
            for group in range(groups):
                source = (t * groups + group) * SLOT
                for view in range(VIEWS):
                    place = group * depth + view * SLOT
                    bands[part * count + t, place:place + SLOT, :] = spread[source:source + SLOT, view * half:(view + 1) * half]

    lane = lax.broadcasted_iota(jnp.int32, (channels, half), 1)
    zero = jnp.zeros((channels, half), jnp.bfloat16)

    def to_right(value):
        return jnp.where(lane == 0, zero, pltpu.roll(value, 1, 1))

    def to_left(value):
        return jnp.where(lane == half - 1, zero, pltpu.roll(value, half - 1, 1))

    step = 2 * half

    def two_frames(ref, frame, rows_of):
        return jnp.concatenate([ref[frame, rows_of, :], ref[frame + 1, rows_of, :]], axis=1)

    def first_dot(group, chunk):
        blocks = min(GROUP, rows + 3 - group * GROUP)
        band = [two_frames(bands, 2 * chunk + tap, slice(group * depth, (group + 1) * depth)) for tap in range(TAPS)]
        return jnp.dot(first_w[:blocks * pair, :], jnp.concatenate(band, axis=0), preferred_element_type=jnp.float32)

    def first_rest(group, chunk, total):
        lanes = slice(chunk * step, (chunk + 1) * step)
        for block in range(total.shape[0] // pair):
            row = group * GROUP + block
            first = total[block * pair:(block + 1) * pair, :].astype(jnp.bfloat16) * live_ref[row:row + 1, lanes].astype(jnp.bfloat16)
            value = 0.5 * first.astype(jnp.float32)
            value = (value + value * jnp.tanh(value)).astype(jnp.bfloat16)
            base = row * VIEWS * channels
            for t in range(2):
                inner = slice(t * half, (t + 1) * half)
                if 1 <= row <= rows + 1 and chunk > 0:
                    held[2 * (chunk - 1) + t, (row - 1) * pair:row * pair, :] = first[:, inner]
                frame = 2 * chunk + t
                act[frame, base:base + channels, :] = to_right(value[channels:, inner])
                act[frame, base + channels:base + 3 * channels, :] = value[:, inner]
                act[frame, base + 3 * channels:base + 4 * channels, :] = to_left(value[:channels, inner])

    def second_dot(row, chunk):
        window = TAPS * VIEWS * channels
        base = row * VIEWS * channels
        source = [two_frames(act, 2 * chunk + tap, slice(base, base + window)) for tap in range(TAPS)]
        return jnp.dot(second_w[...], jnp.concatenate(source, axis=0), preferred_element_type=jnp.float32)

    def second_rest(row, chunk, parts):
        second = parts * live_ref[row + 1:row + 2, (chunk + 1) * step:(chunk + 2) * step]
        first = two_frames(held, 2 * chunk, slice(row * pair, (row + 1) * pair))
        value = (first.astype(jnp.float32) + second).astype(jnp.bfloat16)
        base = row * TAPS * channels
        for t in range(2):
            inner = slice(t * half, (t + 1) * half)
            taps[2 * chunk + t, base:base + channels, :] = to_right(value[channels:, inner])
            taps[2 * chunk + t, base + channels:base + 3 * channels, :] = value[:, inner]

    def down_conv(chunk, first_row, last_row):
        depths = slice(first_row * TAPS * channels, last_row * TAPS * channels)
        return jnp.dot(down_w[:, depths], two_frames(taps, 2 * chunk, depths), preferred_element_type=jnp.float32)

    chunks = frames // 2
    pieces = [(group, chunk) for group in range(groups) for chunk in range(chunks + 1)]
    waiting, final = [], [(rows, part) for part in range(chunks)]
    total = first_dot(*pieces[0])
    for number, (group, chunk) in enumerate(pieces):
        beside = waiting.pop(0) if waiting else None
        parts = second_dot(*beside) if beside else None
        later = first_dot(*pieces[number + 1]) if number + 1 < len(pieces) else None
        first_rest(group, chunk, total)
        if beside:
            second_rest(*beside, parts)
        total = later
        if chunk > 0:
            for row in range(rows):
                if group == (row + 2) // GROUP:
                    waiting.append((row, chunk - 1))
    for row, part in waiting:
        second_rest(row, part, second_dot(row, part))
    early = [down_conv(part, 0, rows) for part in range(chunks)]
    parts = [second_dot(*piece) for piece in final]
    for piece, part in zip(final, parts):
        second_rest(*piece, part)
    size = down_w.shape[0]
    for part in range(chunks):
        encoded = (early[part] + down_conv(part, rows, rows + 1)).astype(jnp.bfloat16)
        for t in range(2):
            frame = part * 2 + t
            out_ref[frame * size:(frame + 1) * size, :] = encoded[:, t * half:(t + 1) * half]


def hbm(array):
    return pltpu.with_memory_space_constraint(array, pltpu.HBM)


def snake(row_devices, frame_devices):
    route = []
    for left in range(0, frame_devices, 2):
        ring = [(row, left) for row in range(row_devices)] + [(row, left + 1) for row in reversed(range(row_devices))]
        ring = [row * frame_devices + frame for row, frame in ring]
        route += list(zip(ring, ring[1:] + ring[:1]))
    return route


def shards(pixels, frame_counts, weight_first, weight_second, weight_down):
    clips, frames, colors, rows, width = pixels.shape
    channels = weight_first.shape[3]
    half = width // 2
    out_rows = rows // 2
    frame_devices, row_devices = lax.axis_size("frames"), lax.axis_size("rows")
    assert clips == 1 and frames >= 4 and rows >= 3 and rows % 2 == 0 and frames % 2 == 0
    assert (GROUP + 2) * colors <= SLOT and frame_devices % 2 == 0
    bf16 = jnp.bfloat16
    frame_device = lax.axis_index("frames")
    size = frames * colors * rows
    earlier = lax.ppermute(pixels[0, -4:], "frames", [(i, (i + 1) % frame_devices) for i in range(frame_devices)])
    late = lax.optimization_barrier(pixels[0].reshape(size, width))
    earlier = earlier.reshape(4 * colors * rows, width)
    earlier = jnp.where(frame_device > 0, earlier, jnp.zeros_like(earlier))
    own = jnp.concatenate([earlier, late], axis=0)
    own, weight_first, frame_counts = lax.optimization_barrier((own, weight_first, frame_counts))
    route = snake(row_devices, frame_devices)
    axes = ("rows", "frames")
    there = lax.ppermute(own, axes, route)
    back = lax.ppermute(own, axes, [(b, a) for a, b in route])

    pair = PARITIES * channels
    wide = (frames + 2) * half
    depth = TAPS * VIEWS * SLOT
    groups = -(-(rows + 3) // GROUP)
    first_w, second_w, down_w, live, gather, columns = pl.pallas_call(
        lambda *refs: prepare_kernel(*refs, rows=rows, frames=frames),
        name="prepare",
        compiler_params=pltpu.CompilerParams(vmem_limit_bytes=8 << 20),
        in_specs=[SMEM] + [HBM] * 3,
        out_specs=[VMEM] * 6,
        out_shape=[
            jax.ShapeDtypeStruct((GROUP * pair, depth), bf16),
            jax.ShapeDtypeStruct((pair, TAPS * TAPS * VIEWS * channels), bf16),
            jax.ShapeDtypeStruct((channels * out_rows, (rows + 1) * TAPS * channels), bf16),
            jax.ShapeDtypeStruct((rows + 3, wide), jnp.float32),
            jax.ShapeDtypeStruct(((frames + 4) // HALVES * groups * SLOT, 3 * own.shape[0] // HALVES), bf16),
            jax.ShapeDtypeStruct((width, VIEWS * half), bf16),
        ],
        scratch_shapes=[
            pltpu.VMEM((TAPS**3, colors, channels), bf16),
            pltpu.VMEM((TAPS**3, channels, channels), bf16),
            pltpu.VMEM((TAPS**2, channels, channels), bf16),
            pltpu.SemaphoreType.DMA((3,)),
        ],
    )(
        frame_counts,
        hbm(weight_first.transpose(0, 1, 2, 4, 3).reshape(TAPS**3, colors, channels)),
        hbm(weight_second.reshape(TAPS**3, channels, channels)),
        hbm(weight_down.reshape(TAPS**2, channels, channels)),
    )
    encoded = pl.pallas_call(
        lambda *refs: encode_kernel(*refs, rows=rows, frames=frames),
        name="encode",
        compiler_params=pltpu.CompilerParams(vmem_limit_bytes=24 << 20),
        in_specs=[VMEM] * 9,
        out_specs=VMEM,
        out_shape=jax.ShapeDtypeStruct((frames * channels * out_rows, half), bf16),
        scratch_shapes=[
            pltpu.VMEM((3 * own.shape[0], width), bf16),
            pltpu.VMEM((frames + 4, groups * VIEWS * SLOT, half), bf16),
            pltpu.VMEM((frames + 2, (rows + 3) * VIEWS * channels, half), bf16),
            pltpu.VMEM((frames, (rows + 1) * pair, half), bf16),
            pltpu.VMEM((frames, (rows + 1) * TAPS * channels, half), bf16),
        ],
    )(own, there, back, gather, columns, live, first_w, second_w, down_w)
    return encoded.reshape(1, frames, channels, out_rows, half)


def solution(mesh):
    in_specs = (
        P(("groups", "clips"), "frames", None, "rows", None),
        P(("groups", "clips")),
        P(),
        P(),
        P(),
    )
    out_specs = P(("groups", "clips"), "frames", None, "rows", None)
    return jax.shard_map(shards, mesh=mesh, in_specs=in_specs, out_specs=out_specs, check_vma=False)
```

```python
import jax
import jax.numpy as jnp
from jax import lax
from jax.experimental import pallas as pl
from jax.experimental.pallas import tpu as pltpu
from jax.sharding import PartitionSpec as P

VIEWS = 4
PARITIES = 2
TAPS = 3
GROUP = 3
SLOT = 16
SUBLANES = 8
HALVES = 2

VMEM = pl.BlockSpec(memory_space=pltpu.VMEM)
HBM = pl.BlockSpec(memory_space=pltpu.HBM)
SMEM = pl.BlockSpec(memory_space=pltpu.SMEM)


def one_hot(shape, target, valid):
    lane = lax.broadcasted_iota(jnp.int32, shape, 1)
    return jnp.where(lane == jnp.where(valid, target, -1), 1.0, 0.0).astype(jnp.bfloat16)


def act_groups(rows):
    apart = [(0, 3), (rows + 1, 2)]
    alone = [(start, min(GROUP, rows + 1 - start)) for start in range(3, rows + 1, GROUP)]
    return apart, alone


def band_targets(size, runs, colors):
    line = lax.broadcasted_iota(jnp.int32, (size, 1), 0)
    frame, run, inner = line // (len(runs) * SLOT), line // SLOT % len(runs), line % SLOT
    start, count = 0, 0
    for number, (first, rows_of) in enumerate(runs):
        start, count = jnp.where(run == number, first, start), jnp.where(run == number, rows_of + 2, count)
    return frame, inner % colors, start + inner // colors - 3, inner < count * colors


def spread_bands(gather, lines, columns, bands, first_frame, runs):
    spread = jnp.dot(gather, lines, preferred_element_type=jnp.float32).astype(jnp.bfloat16)
    spread = jnp.dot(spread, columns, preferred_element_type=jnp.float32).astype(jnp.bfloat16)
    half = bands.shape[2]
    for line in range(spread.shape[0] // SLOT):
        t, run = line // len(runs), line % len(runs)
        for view in range(VIEWS):
            place = (run * VIEWS + view) * SLOT
            bands[first_frame + t, place:place + SLOT, :] = spread[line * SLOT:(line + 1) * SLOT, view * half:(view + 1) * half]


def tap_rows(row, rows, alone):
    return [tap for tap in range(TAPS) if (3 <= row + tap <= rows) == alone]


def second_product(weights, row_source, row, chunk, row_taps):
    channels = weights.shape[0] // PARITIES
    size = VIEWS * channels
    lines, columns = [], []
    for tap_t in range(TAPS):
        for tap_y in row_taps:
            ref, line = row_source(row + tap_y)
            lines.append(two_frames(ref, 2 * chunk + tap_t, slice(line * size, (line + 1) * size)))
            start = (tap_t * TAPS + tap_y) * size
            columns.append(weights[:, start:start + size])
    return jnp.dot(jnp.concatenate(columns, axis=1), jnp.concatenate(lines, axis=0), preferred_element_type=jnp.float32)


def two_frames(ref, frame, rows_of):
    return jnp.concatenate([ref[frame, rows_of, :], ref[frame + 1, rows_of, :]], axis=1)


def to_right(value):
    lane = lax.broadcasted_iota(jnp.int32, value.shape, 1)
    return jnp.where(lane == 0, jnp.zeros_like(value), pltpu.roll(value, 1, 1))


def to_left(value):
    lane = lax.broadcasted_iota(jnp.int32, value.shape, 1)
    return jnp.where(lane == value.shape[1] - 1, jnp.zeros_like(value), pltpu.roll(value, value.shape[1] - 1, 1))


def first_product(weights, bands, run, count, chunk):
    depth = VIEWS * SLOT
    band = [two_frames(bands, 2 * chunk + tap, slice(run * depth, (run + 1) * depth)) for tap in range(TAPS)]
    pair = weights.shape[0] // GROUP
    return jnp.dot(weights[:count * pair, :], jnp.concatenate(band, axis=0), preferred_element_type=jnp.float32)


def activate(total, live, rows_of, chunk, act, held, base_row, rows):
    half = act.shape[2]
    pair = total.shape[0] // len(rows_of)
    channels = pair // PARITIES
    for block, row in enumerate(rows_of):
        mask = live[row:row + 1, 2 * chunk * half:2 * (chunk + 1) * half].astype(jnp.bfloat16)
        first = total[block * pair:(block + 1) * pair, :].astype(jnp.bfloat16) * mask
        value = 0.5 * first.astype(jnp.float32)
        value = (value + value * jnp.tanh(value)).astype(jnp.bfloat16)
        base = (row - base_row) * VIEWS * channels
        for t in range(2):
            inner = slice(t * half, (t + 1) * half)
            if 1 <= row <= rows + 1 and chunk > 0:
                held[2 * (chunk - 1) + t, (row - base_row) * pair:(row - base_row + 1) * pair, :] = first[:, inner]
            frame = 2 * chunk + t
            act[frame, base:base + channels, :] = to_right(value[channels:, inner])
            act[frame, base + channels:base + 3 * channels, :] = value[:, inner]
            act[frame, base + 3 * channels:base + 4 * channels, :] = to_left(value[:channels, inner])


def load_kernel(*refs):
    count = (len(refs) - 1) // 2
    copies = [pltpu.make_async_copy(refs[i], refs[count + i], refs[-1].at[i]) for i in range(count)]
    for copy in copies:
        copy.start()
    for copy in copies:
        copy.wait()


def prepare_kernel(count, own, first, second, down, first_out, second_out, down_out, live_out, gather_out, columns_out, held_out, partial_out, bands, act, *, rows, frames):
    channels = first.shape[2]
    colors = first.shape[1]
    apart, alone = act_groups(rows)

    size = TAPS**3 * SUBLANES
    line = lax.broadcasted_iota(jnp.int32, (size, 1), 0)
    tap, color = line // SUBLANES, line % SUBLANES
    target = (tap // TAPS**2 * VIEWS + tap % TAPS) * SLOT + tap // TAPS % TAPS * colors + color
    chosen = one_hot((size, first_out.shape[1]), target, color < colors)

    width = columns_out.shape[0]
    column = lax.broadcasted_iota(jnp.int32, columns_out.shape, 0)
    place = lax.broadcasted_iota(jnp.int32, columns_out.shape, 1)
    half = width // 2
    columns_out[...] = jnp.where(column == place % half * 2 + place // half - 1, 1.0, 0.0).astype(jnp.bfloat16)

    part = (frames + 4) // HALVES
    size = part * colors * rows
    frame, color, row, used = band_targets(part * len(alone) * SLOT, alone, colors)
    gather = one_hot((part * len(alone) * SLOT, size), (frame * colors + color) * rows + row, used)
    for number in range(HALVES):
        spread_bands(gather, own[number * size:(number + 1) * size, :], columns_out[...], bands, number * part, alone)

    frame = lax.broadcasted_iota(jnp.int32, live_out.shape, 1) // half + (lax.axis_index("frames") * frames - 2)
    row = lax.broadcasted_iota(jnp.int32, live_out.shape, 0) + (lax.axis_index("rows") * rows - 2)
    inside = jnp.logical_and(row >= 0, row < lax.axis_size("rows") * rows)
    live_out[...] = jnp.where(jnp.logical_and(inside, frame < count[0]), 1.0, 0.0)

    filler = jnp.zeros((SUBLANES - colors, channels), jnp.float32)
    lines = []
    for tap in range(TAPS**3):
        lines += [first[tap].astype(jnp.float32), filler]
    lines = jnp.concatenate(lines, axis=0).T.astype(jnp.bfloat16)
    base = jnp.dot(lines, chosen, preferred_element_type=jnp.float32)
    for block in range(GROUP):
        for parity in range(PARITIES):
            shift = parity * SLOT + block * colors
            moved = pltpu.roll(base, shift, 1) if shift else base
            start = (block * PARITIES + parity) * channels
            first_out[start:start + channels, :] = moved.astype(jnp.bfloat16)

    for run, (start, rows_of) in enumerate(alone):
        for chunk in range(frames // 2 + 1):
            total = first_product(first_out, bands, run, rows_of, chunk)
            activate(total, live_out, range(start, start + rows_of), chunk, act, held_out, 3, rows)

    odd = lax.rem(lax.axis_index("frames"), 2)
    frame, color, row, used = band_targets(gather_out.shape[0], apart, colors)
    source = jnp.where(row < 0, 1 + odd, jnp.where(row < rows, 0, 2 - odd))
    local = jnp.where(row < 0, row + rows, jnp.where(row < rows, row, row - rows))
    gather_out[...] = one_hot(gather_out.shape, ((source * part + frame) * colors + color) * rows + local, used)

    none = jnp.zeros((channels, channels), jnp.bfloat16)
    for tap in range(TAPS * TAPS):
        taps = [second[tap * TAPS + tap_x] for tap_x in range(TAPS)]
        columns = slice(tap * VIEWS * channels, (tap + 1) * VIEWS * channels)
        second_out[:channels, columns] = jnp.concatenate(taps + [none], axis=1)
        second_out[channels:, columns] = jnp.concatenate([none] + taps, axis=1)

    for row in range(1, rows + 1):
        for chunk in range(frames // 2):
            partial_out[row - 1, chunk] = second_product(second_out, lambda line: (act, line - 3), row, chunk, tap_rows(row, rows, True))

    out_rows = down_out.shape[0] // channels
    sum_rows = down_out.shape[1] // (TAPS * channels)
    taps = jnp.concatenate([down[tap] for tap in range(TAPS * TAPS)], axis=1)
    place = lax.broadcasted_iota(jnp.int32, (down_out.shape[0], channels), 0)
    channel = lax.broadcasted_iota(jnp.int32, (down_out.shape[0], channels), 1)
    total = None
    for y in range(out_rows):
        spread = (place == channel * out_rows + y).astype(jnp.float32).astype(jnp.bfloat16)
        pieces = [taps]
        before, after = 2 * y, sum_rows - TAPS - 2 * y
        if before:
            pieces = [jnp.zeros((channels, before * TAPS * channels), jnp.bfloat16)] + pieces
        if after:
            pieces = pieces + [jnp.zeros((channels, after * TAPS * channels), jnp.bfloat16)]
        part = jnp.dot(spread, jnp.concatenate(pieces, axis=1), preferred_element_type=jnp.float32)
        total = part if total is None else total + part
    down_out[...] = total.astype(jnp.bfloat16)


def encode_kernel(own_ref, there_ref, back_ref, gather_ref, columns_ref, live_ref, held_own, partial_ref, first_w, second_w, down_w, out_ref, lines, bands, act, held, taps, *, rows, frames):
    half = columns_ref.shape[1] // VIEWS
    channels = second_w.shape[0] // PARITIES
    pair = PARITIES * channels
    apart, _ = act_groups(rows)
    odd = lax.rem(lax.axis_index("frames"), 2)
    row_device = lax.axis_index("rows")
    top, bottom = row_device == 0, row_device == lax.axis_size("rows") - 1
    keep_there = jnp.where(jnp.logical_or(jnp.logical_and(odd == 0, top), jnp.logical_and(odd == 1, bottom)), 0.0, 1.0).astype(jnp.bfloat16)
    keep_back = jnp.where(jnp.logical_or(jnp.logical_and(odd == 1, top), jnp.logical_and(odd == 0, bottom)), 0.0, 1.0).astype(jnp.bfloat16)
    size = own_ref.shape[0] // HALVES
    for part in range(HALVES):
        rows_of = slice(part * size, (part + 1) * size)
        base = part * 3 * size
        lines[base:base + size, :] = own_ref[rows_of, :]
        lines[base + size:base + 2 * size, :] = there_ref[rows_of, :] * keep_there
        lines[base + 2 * size:base + 3 * size, :] = back_ref[rows_of, :] * keep_back
        spread_bands(gather_ref[...], lines[base:base + 3 * size, :], columns_ref[...], bands, part * (frames + 4) // HALVES, apart)

    step = 2 * half
    chunks = frames // 2

    def second_dot(row, chunk):
        total = second_product(second_w, lambda line: (act, line), row, chunk, tap_rows(row, rows, False))
        return total + partial_ref[row - 1, chunk] if row > 0 else total

    def second_rest(row, chunk, total):
        second = total * live_ref[row + 1:row + 2, (chunk + 1) * step:(chunk + 2) * step]
        source, base = (held_own, row - 2) if 3 <= row + 1 <= rows else (held, row + 1)
        first = two_frames(source, 2 * chunk, slice(base * pair, (base + 1) * pair))
        value = (first.astype(jnp.float32) + second).astype(jnp.bfloat16)
        base = row * TAPS * channels
        for t in range(2):
            inner = slice(t * half, (t + 1) * half)
            taps[2 * chunk + t, base:base + channels, :] = to_right(value[channels:, inner])
            taps[2 * chunk + t, base + channels:base + 3 * channels, :] = value[:, inner]

    def down_conv(chunk, first_row, last_row):
        depths = slice(first_row * TAPS * channels, last_row * TAPS * channels)
        return jnp.dot(down_w[:, depths], two_frames(taps, 2 * chunk, depths), preferred_element_type=jnp.float32)

    pieces = [(run, chunk) for run in range(len(apart)) for chunk in range(chunks + 1)]
    waiting = []
    total = first_product(first_w, bands, pieces[0][0], apart[pieces[0][0]][1], pieces[0][1])
    for number, (run, chunk) in enumerate(pieces):
        beside = waiting.pop(0) if waiting else None
        parts = second_dot(*beside) if beside else None
        if number + 1 < len(pieces):
            later_run, later_chunk = pieces[number + 1]
            later = first_product(first_w, bands, later_run, apart[later_run][1], later_chunk)
        start, count = apart[run]
        activate(total, live_ref, range(start, start + count), chunk, act, held, 0, rows)
        if beside:
            second_rest(*beside, parts)
        total = later
        if chunk > 0:
            ready = [row for row in range(rows) if (row + 2 > rows) == (run > 0)]
            waiting += [(row, chunk - 1) for row in ready]
    for row, part in waiting:
        second_rest(row, part, second_dot(row, part))
    early = [down_conv(part, 0, rows) for part in range(chunks)]
    parts = [second_dot(rows, part) for part in range(chunks)]
    for part in range(chunks):
        second_rest(rows, part, parts[part])
    size = down_w.shape[0]
    for part in range(chunks):
        encoded = (early[part] + down_conv(part, rows, rows + 1)).astype(jnp.bfloat16)
        for t in range(2):
            frame = part * 2 + t
            out_ref[frame * size:(frame + 1) * size, :] = encoded[:, t * half:(t + 1) * half]


def hbm(array):
    return pltpu.with_memory_space_constraint(array, pltpu.HBM)


def snake(row_devices, frame_devices):
    route = []
    for left in range(0, frame_devices, 2):
        ring = [(row, left) for row in range(row_devices)] + [(row, left + 1) for row in reversed(range(row_devices))]
        ring = [row * frame_devices + frame for row, frame in ring]
        route += list(zip(ring, ring[1:] + ring[:1]))
    return route


def shards(pixels, frame_counts, weight_first, weight_second, weight_down):
    clips, frames, colors, rows, width = pixels.shape
    channels = weight_first.shape[3]
    half = width // 2
    out_rows = rows // 2
    frame_devices, row_devices = lax.axis_size("frames"), lax.axis_size("rows")
    assert clips == 1 and frames >= 4 and rows >= 3 and rows % 2 == 0 and frames % 2 == 0
    assert (GROUP + 2) * colors <= SLOT and frame_devices % 2 == 0
    bf16 = jnp.bfloat16
    frame_device = lax.axis_index("frames")
    size = frames * colors * rows
    earlier = lax.ppermute(pixels[0, -4:], "frames", [(i, (i + 1) % frame_devices) for i in range(frame_devices)])
    arrays = [
        hbm(pixels[0]),
        hbm(weight_first.transpose(0, 1, 2, 4, 3).reshape(TAPS**3, colors, channels)),
        hbm(weight_second.reshape(TAPS**3, channels, channels)),
        hbm(weight_down.reshape(TAPS**2, channels, channels)),
    ]
    loaded, weight_first, weight_second, weight_down = pl.pallas_call(
        load_kernel,
        name="load",
        compiler_params=pltpu.CompilerParams(vmem_limit_bytes=8 << 20),
        in_specs=[HBM] * len(arrays),
        out_specs=[VMEM] * len(arrays),
        out_shape=[jax.ShapeDtypeStruct(array.shape, bf16) for array in arrays],
        scratch_shapes=[pltpu.SemaphoreType.DMA((len(arrays),))],
    )(*arrays)
    late = loaded.reshape(size, width)
    earlier = earlier.reshape(4 * colors * rows, width)
    earlier = jnp.where(frame_device > 0, earlier, jnp.zeros_like(earlier))
    own = jnp.concatenate([earlier, late], axis=0)
    own, frame_counts = lax.optimization_barrier((own, frame_counts))
    route = snake(row_devices, frame_devices)
    axes = ("rows", "frames")
    back = lax.ppermute(own, axes, [(b, a) for a, b in route])
    there = lax.ppermute(own, axes, route)

    pair = PARITIES * channels
    wide = (frames + 2) * half
    depth = VIEWS * SLOT
    part = (frames + 4) // HALVES
    apart, alone = act_groups(rows)
    first_w, second_w, down_w, live, gather, columns, held_own, partial = pl.pallas_call(
        lambda *refs: prepare_kernel(*refs, rows=rows, frames=frames),
        name="prepare",
        compiler_params=pltpu.CompilerParams(vmem_limit_bytes=12 << 20),
        in_specs=[SMEM] + [VMEM] * 4,
        out_specs=[VMEM] * 8,
        out_shape=[
            jax.ShapeDtypeStruct((GROUP * pair, TAPS * depth), bf16),
            jax.ShapeDtypeStruct((pair, TAPS * TAPS * VIEWS * channels), bf16),
            jax.ShapeDtypeStruct((channels * out_rows, (rows + 1) * TAPS * channels), bf16),
            jax.ShapeDtypeStruct((rows + 3, wide), jnp.float32),
            jax.ShapeDtypeStruct((part * len(apart) * SLOT, 3 * own.shape[0] // HALVES), bf16),
            jax.ShapeDtypeStruct((width, VIEWS * half), bf16),
            jax.ShapeDtypeStruct((frames, (rows - 2) * pair, half), bf16),
            jax.ShapeDtypeStruct((rows, frames // 2, pair, 2 * half), jnp.float32),
        ],
        scratch_shapes=[
            pltpu.VMEM((frames + 4, len(alone) * depth, half), bf16),
            pltpu.VMEM((frames + 2, (rows - 2) * VIEWS * channels, half), bf16),
        ],
    )(frame_counts, own, weight_first, weight_second, weight_down)
    encoded = pl.pallas_call(
        lambda *refs: encode_kernel(*refs, rows=rows, frames=frames),
        name="encode",
        compiler_params=pltpu.CompilerParams(vmem_limit_bytes=24 << 20),
        in_specs=[VMEM] * 11,
        out_specs=VMEM,
        out_shape=jax.ShapeDtypeStruct((frames * channels * out_rows, half), bf16),
        scratch_shapes=[
            pltpu.VMEM((3 * own.shape[0], width), bf16),
            pltpu.VMEM((frames + 4, len(apart) * depth, half), bf16),
            pltpu.VMEM((frames + 2, (rows + 3) * VIEWS * channels, half), bf16),
            pltpu.VMEM((frames, (rows + 3) * pair, half), bf16),
            pltpu.VMEM((frames, (rows + 1) * TAPS * channels, half), bf16),
        ],
    )(own, there, back, gather, columns, live, held_own, partial, first_w, second_w, down_w)
    return encoded.reshape(1, frames, channels, out_rows, half)


def solution(mesh):
    in_specs = (
        P(("groups", "clips"), "frames", None, "rows", None),
        P(("groups", "clips")),
        P(),
        P(),
        P(),
    )
    out_specs = P(("groups", "clips"), "frames", None, "rows", None)
    return jax.shard_map(shards, mesh=mesh, in_specs=in_specs, out_specs=out_specs, check_vma=False)
```

```python
import jax
import jax.numpy as jnp
from jax import lax
from jax.experimental import pallas as pl
from jax.experimental.pallas import tpu as pltpu
from jax.sharding import PartitionSpec as P

VIEWS = 4
PARITIES = 2
TAPS = 3
GROUP = 3
SLOT = 16
SUBLANES = 8
HALVES = 2

VMEM = pl.BlockSpec(memory_space=pltpu.VMEM)
HBM = pl.BlockSpec(memory_space=pltpu.HBM)
SMEM = pl.BlockSpec(memory_space=pltpu.SMEM)


def one_hot(shape, target, valid):
    lane = lax.broadcasted_iota(jnp.int32, shape, 1)
    return jnp.where(lane == jnp.where(valid, target, -1), 1.0, 0.0).astype(jnp.bfloat16)


def act_groups(rows):
    apart = [(0, 3), (rows + 1, 2)]
    alone = [(start, min(GROUP, rows + 1 - start)) for start in range(3, rows + 1, GROUP)]
    return apart, alone


def band_targets(size, runs, colors):
    line = lax.broadcasted_iota(jnp.int32, (size, 1), 0)
    frame, run, inner = line // (len(runs) * SLOT), line // SLOT % len(runs), line % SLOT
    start, count = 0, 0
    for number, (first, rows_of) in enumerate(runs):
        start, count = jnp.where(run == number, first, start), jnp.where(run == number, rows_of + 2, count)
    return frame, inner % colors, start + inner // colors - 3, inner < count * colors


def spread_bands(gather, lines, columns, bands, first_frame, runs):
    spread = jnp.dot(gather, lines, preferred_element_type=jnp.float32).astype(jnp.bfloat16)
    spread = jnp.dot(spread, columns, preferred_element_type=jnp.float32).astype(jnp.bfloat16)
    half = bands.shape[2]
    for line in range(spread.shape[0] // SLOT):
        t, run = line // len(runs), line % len(runs)
        for view in range(VIEWS):
            place = (run * VIEWS + view) * SLOT
            bands[first_frame + t, place:place + SLOT, :] = spread[line * SLOT:(line + 1) * SLOT, view * half:(view + 1) * half]


def tap_rows(row, rows, alone):
    return [tap for tap in range(TAPS) if (3 <= row + tap <= rows) == alone]


def second_product(weights, row_source, row, chunk, row_taps):
    channels = weights.shape[0] // PARITIES
    size = VIEWS * channels
    lines, columns = [], []
    for tap_t in range(TAPS):
        for tap_y in row_taps:
            ref, line = row_source(row + tap_y)
            lines.append(two_frames(ref, 2 * chunk + tap_t, slice(line * size, (line + 1) * size)))
            start = (tap_t * TAPS + tap_y) * size
            columns.append(weights[:, start:start + size])
    return jnp.dot(jnp.concatenate(columns, axis=1), jnp.concatenate(lines, axis=0), preferred_element_type=jnp.float32)


def two_frames(ref, frame, rows_of):
    return jnp.concatenate([ref[frame, rows_of, :], ref[frame + 1, rows_of, :]], axis=1)


def to_right(value):
    lane = lax.broadcasted_iota(jnp.int32, value.shape, 1)
    return jnp.where(lane == 0, jnp.zeros_like(value), pltpu.roll(value, 1, 1))


def to_left(value):
    lane = lax.broadcasted_iota(jnp.int32, value.shape, 1)
    return jnp.where(lane == value.shape[1] - 1, jnp.zeros_like(value), pltpu.roll(value, value.shape[1] - 1, 1))


def first_product(weights, bands, run, count, chunk):
    depth = VIEWS * SLOT
    band = [two_frames(bands, 2 * chunk + tap, slice(run * depth, (run + 1) * depth)) for tap in range(TAPS)]
    pair = weights.shape[0] // GROUP
    return jnp.dot(weights[:count * pair, :], jnp.concatenate(band, axis=0), preferred_element_type=jnp.float32)


def activate(total, live, rows_of, chunk, act, held, base_row, rows):
    half = act.shape[2]
    pair = total.shape[0] // len(rows_of)
    channels = pair // PARITIES
    for block, row in enumerate(rows_of):
        mask = live[row:row + 1, 2 * chunk * half:2 * (chunk + 1) * half].astype(jnp.bfloat16)
        first = total[block * pair:(block + 1) * pair, :].astype(jnp.bfloat16) * mask
        value = 0.5 * first.astype(jnp.float32)
        value = (value + value * jnp.tanh(value)).astype(jnp.bfloat16)
        base = (row - base_row) * VIEWS * channels
        for t in range(2):
            inner = slice(t * half, (t + 1) * half)
            if 1 <= row <= rows + 1 and chunk > 0:
                held[2 * (chunk - 1) + t, (row - base_row) * pair:(row - base_row + 1) * pair, :] = first[:, inner]
            frame = 2 * chunk + t
            act[frame, base:base + channels, :] = to_right(value[channels:, inner])
            act[frame, base + channels:base + 3 * channels, :] = value[:, inner]
            act[frame, base + 3 * channels:base + 4 * channels, :] = to_left(value[:channels, inner])


def load_kernel(pixels_hbm, first_hbm, second_hbm, down_hbm, pixels, first, second, down, chosen, columns_out, gather_own, gather_out, sems, *, rows, frames):
    arrays = ((pixels_hbm, pixels), (first_hbm, first), (second_hbm, second), (down_hbm, down))
    copies = [pltpu.make_async_copy(source, target, sems.at[i]) for i, (source, target) in enumerate(arrays)]
    for copy in copies:
        copy.start()
    colors = pixels.shape[1]
    apart, alone = act_groups(rows)
    part = (frames + 4) // HALVES

    size = TAPS**3 * SUBLANES
    line = lax.broadcasted_iota(jnp.int32, (size, 1), 0)
    tap, color = line // SUBLANES, line % SUBLANES
    target = (tap // TAPS**2 * VIEWS + tap % TAPS) * SLOT + tap // TAPS % TAPS * colors + color
    chosen[...] = one_hot(chosen.shape, target, color < colors)

    width = columns_out.shape[0]
    column = lax.broadcasted_iota(jnp.int32, columns_out.shape, 0)
    place = lax.broadcasted_iota(jnp.int32, columns_out.shape, 1)
    half = width // 2
    columns_out[...] = jnp.where(column == place % half * 2 + place // half - 1, 1.0, 0.0).astype(jnp.bfloat16)

    frame, color, row, used = band_targets(gather_own.shape[0], alone, colors)
    gather_own[...] = one_hot(gather_own.shape, (frame * colors + color) * rows + row, used)

    odd = lax.rem(lax.axis_index("frames"), 2)
    frame, color, row, used = band_targets(gather_out.shape[0], apart, colors)
    source = jnp.where(row < 0, 1 + odd, jnp.where(row < rows, 0, 2 - odd))
    local = jnp.where(row < 0, row + rows, jnp.where(row < rows, row, row - rows))
    gather_out[...] = one_hot(gather_out.shape, ((source * part + frame) * colors + color) * rows + local, used)

    for copy in copies:
        copy.wait()


def prepare_kernel(count, own, first, second, down, chosen, columns, gather, first_out, second_out, down_out, live_out, held_out, partial_out, bands, act, *, rows, frames):
    channels = first.shape[2]
    colors = first.shape[1]
    _, alone = act_groups(rows)
    half = columns.shape[1] // VIEWS

    none = jnp.zeros((channels, channels), jnp.bfloat16)
    for tap in range(TAPS * TAPS):
        taps = [second[tap * TAPS + tap_x] for tap_x in range(TAPS)]
        depths = slice(tap * VIEWS * channels, (tap + 1) * VIEWS * channels)
        second_out[:channels, depths] = jnp.concatenate(taps + [none], axis=1)
        second_out[channels:, depths] = jnp.concatenate([none] + taps, axis=1)

    part = (frames + 4) // HALVES
    size = part * colors * rows
    for number in range(HALVES):
        spread_bands(gather[...], own[number * size:(number + 1) * size, :], columns[...], bands, number * part, alone)

    frame = lax.broadcasted_iota(jnp.int32, live_out.shape, 1) // half + (lax.axis_index("frames") * frames - 2)
    row = lax.broadcasted_iota(jnp.int32, live_out.shape, 0) + (lax.axis_index("rows") * rows - 2)
    inside = jnp.logical_and(row >= 0, row < lax.axis_size("rows") * rows)
    live_out[...] = jnp.where(jnp.logical_and(inside, frame < count[0]), 1.0, 0.0)

    filler = jnp.zeros((SUBLANES - colors, channels), jnp.float32)
    lines = []
    for tap in range(TAPS**3):
        lines += [first[tap].astype(jnp.float32), filler]
    lines = jnp.concatenate(lines, axis=0).T.astype(jnp.bfloat16)
    base = jnp.dot(lines, chosen[...], preferred_element_type=jnp.float32)
    for block in range(GROUP):
        for parity in range(PARITIES):
            shift = parity * SLOT + block * colors
            moved = pltpu.roll(base, shift, 1) if shift else base
            start = (block * PARITIES + parity) * channels
            first_out[start:start + channels, :] = moved.astype(jnp.bfloat16)

    for run, (start, rows_of) in enumerate(alone):
        for chunk in range(frames // 2 + 1):
            total = first_product(first_out, bands, run, rows_of, chunk)
            activate(total, live_out, range(start, start + rows_of), chunk, act, held_out, 3, rows)

    for row in range(1, rows + 1):
        for chunk in range(frames // 2):
            partial_out[row - 1, chunk] = second_product(second_out, lambda line: (act, line - 3), row, chunk, tap_rows(row, rows, True))

    out_rows = down_out.shape[0] // channels
    sum_rows = down_out.shape[1] // (TAPS * channels)
    taps = jnp.concatenate([down[tap] for tap in range(TAPS * TAPS)], axis=1)
    place = lax.broadcasted_iota(jnp.int32, (down_out.shape[0], channels), 0)
    channel = lax.broadcasted_iota(jnp.int32, (down_out.shape[0], channels), 1)
    total = None
    for y in range(out_rows):
        spread = (place == channel * out_rows + y).astype(jnp.float32).astype(jnp.bfloat16)
        pieces = [taps]
        before, after = 2 * y, sum_rows - TAPS - 2 * y
        if before:
            pieces = [jnp.zeros((channels, before * TAPS * channels), jnp.bfloat16)] + pieces
        if after:
            pieces = pieces + [jnp.zeros((channels, after * TAPS * channels), jnp.bfloat16)]
        part = jnp.dot(spread, jnp.concatenate(pieces, axis=1), preferred_element_type=jnp.float32)
        total = part if total is None else total + part
    down_out[...] = total.astype(jnp.bfloat16)


def encode_kernel(own_ref, there_ref, back_ref, gather_ref, columns_ref, live_ref, held_own, partial_ref, first_w, second_w, down_w, out_ref, lines, bands, act, held, taps, *, rows, frames):
    half = columns_ref.shape[1] // VIEWS
    channels = second_w.shape[0] // PARITIES
    pair = PARITIES * channels
    apart, _ = act_groups(rows)
    odd = lax.rem(lax.axis_index("frames"), 2)
    row_device = lax.axis_index("rows")
    top, bottom = row_device == 0, row_device == lax.axis_size("rows") - 1
    keep_there = jnp.where(jnp.logical_or(jnp.logical_and(odd == 0, top), jnp.logical_and(odd == 1, bottom)), 0.0, 1.0).astype(jnp.bfloat16)
    keep_back = jnp.where(jnp.logical_or(jnp.logical_and(odd == 1, top), jnp.logical_and(odd == 0, bottom)), 0.0, 1.0).astype(jnp.bfloat16)
    size = own_ref.shape[0] // HALVES
    for part in range(HALVES):
        rows_of = slice(part * size, (part + 1) * size)
        base = part * 3 * size
        lines[base:base + size, :] = own_ref[rows_of, :]
        lines[base + size:base + 2 * size, :] = there_ref[rows_of, :] * keep_there
        lines[base + 2 * size:base + 3 * size, :] = back_ref[rows_of, :] * keep_back
        spread_bands(gather_ref[...], lines[base:base + 3 * size, :], columns_ref[...], bands, part * (frames + 4) // HALVES, apart)

    step = 2 * half
    chunks = frames // 2

    def second_dot(row, chunk):
        total = second_product(second_w, lambda line: (act, line), row, chunk, tap_rows(row, rows, False))
        return total + partial_ref[row - 1, chunk] if row > 0 else total

    def second_rest(row, chunk, total):
        second = total * live_ref[row + 1:row + 2, (chunk + 1) * step:(chunk + 2) * step]
        source, base = (held_own, row - 2) if 3 <= row + 1 <= rows else (held, row + 1)
        first = two_frames(source, 2 * chunk, slice(base * pair, (base + 1) * pair))
        value = (first.astype(jnp.float32) + second).astype(jnp.bfloat16)
        base = row * TAPS * channels
        for t in range(2):
            inner = slice(t * half, (t + 1) * half)
            taps[2 * chunk + t, base:base + channels, :] = to_right(value[channels:, inner])
            taps[2 * chunk + t, base + channels:base + 3 * channels, :] = value[:, inner]

    def down_conv(chunk, first_row, last_row):
        depths = slice(first_row * TAPS * channels, last_row * TAPS * channels)
        return jnp.dot(down_w[:, depths], two_frames(taps, 2 * chunk, depths), preferred_element_type=jnp.float32)

    pieces = [(run, chunk) for run in range(len(apart)) for chunk in range(chunks + 1)]
    waiting = []
    total = first_product(first_w, bands, pieces[0][0], apart[pieces[0][0]][1], pieces[0][1])
    for number, (run, chunk) in enumerate(pieces):
        beside = waiting.pop(0) if waiting else None
        parts = second_dot(*beside) if beside else None
        if number + 1 < len(pieces):
            later_run, later_chunk = pieces[number + 1]
            later = first_product(first_w, bands, later_run, apart[later_run][1], later_chunk)
        start, count = apart[run]
        activate(total, live_ref, range(start, start + count), chunk, act, held, 0, rows)
        if beside:
            second_rest(*beside, parts)
        total = later
        if chunk > 0:
            ready = [row for row in range(rows) if (row + 2 > rows) == (run > 0)]
            waiting += [(row, chunk - 1) for row in ready]
    for row, part in waiting:
        second_rest(row, part, second_dot(row, part))
    early = [down_conv(part, 0, rows) for part in range(chunks)]
    parts = [second_dot(rows, part) for part in range(chunks)]
    for part in range(chunks):
        second_rest(rows, part, parts[part])
    size = down_w.shape[0]
    for part in range(chunks):
        encoded = (early[part] + down_conv(part, rows, rows + 1)).astype(jnp.bfloat16)
        for t in range(2):
            frame = part * 2 + t
            out_ref[frame * size:(frame + 1) * size, :] = encoded[:, t * half:(t + 1) * half]


def hbm(array):
    return pltpu.with_memory_space_constraint(array, pltpu.HBM)


def snake(row_devices, frame_devices):
    route = []
    for left in range(0, frame_devices, 2):
        ring = [(row, left) for row in range(row_devices)] + [(row, left + 1) for row in reversed(range(row_devices))]
        ring = [row * frame_devices + frame for row, frame in ring]
        route += list(zip(ring, ring[1:] + ring[:1]))
    return route


def shards(pixels, frame_counts, weight_first, weight_second, weight_down):
    clips, frames, colors, rows, width = pixels.shape
    channels = weight_first.shape[3]
    half = width // 2
    out_rows = rows // 2
    frame_devices, row_devices = lax.axis_size("frames"), lax.axis_size("rows")
    assert clips == 1 and frames >= 4 and rows >= 3 and rows % 2 == 0 and frames % 2 == 0
    assert (GROUP + 2) * colors <= SLOT and frame_devices % 2 == 0
    bf16 = jnp.bfloat16
    frame_device = lax.axis_index("frames")
    size = frames * colors * rows
    earlier = lax.ppermute(pixels[0, -4:], "frames", [(i, (i + 1) % frame_devices) for i in range(frame_devices)])
    arrays = [
        hbm(pixels[0]),
        hbm(weight_first.transpose(0, 1, 2, 4, 3).reshape(TAPS**3, colors, channels)),
        hbm(weight_second.reshape(TAPS**3, channels, channels)),
        hbm(weight_down.reshape(TAPS**2, channels, channels)),
    ]
    apart, alone = act_groups(rows)
    part = (frames + 4) // HALVES
    lines = part * colors * rows
    shapes = [array.shape for array in arrays] + [
        (TAPS**3 * SUBLANES, TAPS * VIEWS * SLOT),
        (width, VIEWS * half),
        (part * len(alone) * SLOT, lines),
        (part * len(apart) * SLOT, 3 * lines),
    ]
    loaded, weight_first, weight_second, weight_down, chosen, columns, gather_own, gather = pl.pallas_call(
        lambda *refs: load_kernel(*refs, rows=rows, frames=frames),
        name="load",
        compiler_params=pltpu.CompilerParams(vmem_limit_bytes=8 << 20),
        in_specs=[HBM] * len(arrays),
        out_specs=[VMEM] * len(shapes),
        out_shape=[jax.ShapeDtypeStruct(shape, bf16) for shape in shapes],
        scratch_shapes=[pltpu.SemaphoreType.DMA((len(arrays),))],
    )(*arrays)
    late = loaded.reshape(size, width)
    earlier = earlier.reshape(4 * colors * rows, width)
    earlier = jnp.where(frame_device > 0, earlier, jnp.zeros_like(earlier))
    own = jnp.concatenate([earlier, late], axis=0)
    own, frame_counts = lax.optimization_barrier((own, frame_counts))
    route = snake(row_devices, frame_devices)
    axes = ("rows", "frames")
    back = lax.ppermute(own, axes, [(b, a) for a, b in route])
    there = lax.ppermute(own, axes, route)

    pair = PARITIES * channels
    wide = (frames + 2) * half
    depth = VIEWS * SLOT
    first_w, second_w, down_w, live, held_own, partial = pl.pallas_call(
        lambda *refs: prepare_kernel(*refs, rows=rows, frames=frames),
        name="prepare",
        compiler_params=pltpu.CompilerParams(vmem_limit_bytes=12 << 20),
        in_specs=[SMEM] + [VMEM] * 7,
        out_specs=[VMEM] * 6,
        out_shape=[
            jax.ShapeDtypeStruct((GROUP * pair, TAPS * depth), bf16),
            jax.ShapeDtypeStruct((pair, TAPS * TAPS * VIEWS * channels), bf16),
            jax.ShapeDtypeStruct((channels * out_rows, (rows + 1) * TAPS * channels), bf16),
            jax.ShapeDtypeStruct((rows + 3, wide), jnp.float32),
            jax.ShapeDtypeStruct((frames, (rows - 2) * pair, half), bf16),
            jax.ShapeDtypeStruct((rows, frames // 2, pair, 2 * half), jnp.float32),
        ],
        scratch_shapes=[
            pltpu.VMEM((frames + 4, len(alone) * depth, half), bf16),
            pltpu.VMEM((frames + 2, (rows - 2) * VIEWS * channels, half), bf16),
        ],
    )(frame_counts, own, weight_first, weight_second, weight_down, chosen, columns, gather_own)
    encoded = pl.pallas_call(
        lambda *refs: encode_kernel(*refs, rows=rows, frames=frames),
        name="encode",
        compiler_params=pltpu.CompilerParams(vmem_limit_bytes=24 << 20),
        in_specs=[VMEM] * 11,
        out_specs=VMEM,
        out_shape=jax.ShapeDtypeStruct((frames * channels * out_rows, half), bf16),
        scratch_shapes=[
            pltpu.VMEM((3 * own.shape[0], width), bf16),
            pltpu.VMEM((frames + 4, len(apart) * depth, half), bf16),
            pltpu.VMEM((frames + 2, (rows + 3) * VIEWS * channels, half), bf16),
            pltpu.VMEM((frames, (rows + 3) * pair, half), bf16),
            pltpu.VMEM((frames, (rows + 1) * TAPS * channels, half), bf16),
        ],
    )(own, there, back, gather, columns, live, held_own, partial, first_w, second_w, down_w)
    return encoded.reshape(1, frames, channels, out_rows, half)


def solution(mesh):
    in_specs = (
        P(("groups", "clips"), "frames", None, "rows", None),
        P(("groups", "clips")),
        P(),
        P(),
        P(),
    )
    out_specs = P(("groups", "clips"), "frames", None, "rows", None)
    return jax.shard_map(shards, mesh=mesh, in_specs=in_specs, out_specs=out_specs, check_vma=False)
```

```python
import jax
import jax.numpy as jnp
from jax import lax
from jax.experimental import pallas as pl
from jax.experimental.pallas import tpu as pltpu
from jax.sharding import PartitionSpec as P

VIEWS = 4
PARITIES = 2
TAPS = 3
GROUP = 3
SLOT = 16
SUBLANES = 8
HALVES = 2

VMEM = pl.BlockSpec(memory_space=pltpu.VMEM)
HBM = pl.BlockSpec(memory_space=pltpu.HBM)
SMEM = pl.BlockSpec(memory_space=pltpu.SMEM)


def one_hot(shape, target, valid):
    lane = lax.broadcasted_iota(jnp.int32, shape, 1)
    return jnp.where(lane == jnp.where(valid, target, -1), 1.0, 0.0).astype(jnp.bfloat16)


def act_groups(rows):
    apart = [(0, 3), (rows + 1, 2)]
    alone = [(start, min(GROUP, rows + 1 - start)) for start in range(3, rows + 1, GROUP)]
    return apart, alone


def band_targets(size, runs, colors):
    line = lax.broadcasted_iota(jnp.int32, (size, 1), 0)
    frame, run, inner = line // (len(runs) * SLOT), line // SLOT % len(runs), line % SLOT
    start, count = 0, 0
    for number, (first, rows_of) in enumerate(runs):
        start, count = jnp.where(run == number, first, start), jnp.where(run == number, rows_of + 2, count)
    return frame, inner % colors, start + inner // colors - 3, inner < count * colors


def spread_bands(gather, lines, columns, bands, first_frame, runs):
    spread = jnp.dot(gather, lines, preferred_element_type=jnp.float32).astype(jnp.bfloat16)
    spread = jnp.dot(spread, columns, preferred_element_type=jnp.float32).astype(jnp.bfloat16)
    half = bands.shape[2]
    for line in range(spread.shape[0] // SLOT):
        t, run = line // len(runs), line % len(runs)
        for view in range(VIEWS):
            place = (run * VIEWS + view) * SLOT
            bands[first_frame + t, place:place + SLOT, :] = spread[line * SLOT:(line + 1) * SLOT, view * half:(view + 1) * half]


def tap_rows(row, rows, alone):
    return [tap for tap in range(TAPS) if (3 <= row + tap <= rows) == alone]


def second_product(weights, row_source, row, chunk, row_taps):
    channels = weights.shape[0] // PARITIES
    size = VIEWS * channels
    lines, columns = [], []
    for tap_t in range(TAPS):
        for tap_y in row_taps:
            ref, line = row_source(row + tap_y)
            lines.append(two_frames(ref, 2 * chunk + tap_t, slice(line * size, (line + 1) * size)))
            start = (tap_t * TAPS + tap_y) * size
            columns.append(weights[:, start:start + size])
    return jnp.dot(jnp.concatenate(columns, axis=1), jnp.concatenate(lines, axis=0), preferred_element_type=jnp.float32)


def two_frames(ref, frame, rows_of):
    return jnp.concatenate([ref[frame, rows_of, :], ref[frame + 1, rows_of, :]], axis=1)


def to_right(value):
    lane = lax.broadcasted_iota(jnp.int32, value.shape, 1)
    return jnp.where(lane == 0, jnp.zeros_like(value), pltpu.roll(value, 1, 1))


def to_left(value):
    lane = lax.broadcasted_iota(jnp.int32, value.shape, 1)
    return jnp.where(lane == value.shape[1] - 1, jnp.zeros_like(value), pltpu.roll(value, value.shape[1] - 1, 1))


def first_product(weights, bands, run, count, chunk):
    depth = VIEWS * SLOT
    band = [two_frames(bands, 2 * chunk + tap, slice(run * depth, (run + 1) * depth)) for tap in range(TAPS)]
    pair = weights.shape[0] // GROUP
    return jnp.dot(weights[:count * pair, :], jnp.concatenate(band, axis=0), preferred_element_type=jnp.float32)


def activate(total, live, rows_of, chunk, act, held, base_row, rows):
    half = act.shape[2]
    pair = total.shape[0] // len(rows_of)
    channels = pair // PARITIES
    for block, row in enumerate(rows_of):
        mask = live[row:row + 1, 2 * chunk * half:2 * (chunk + 1) * half].astype(jnp.bfloat16)
        first = total[block * pair:(block + 1) * pair, :].astype(jnp.bfloat16) * mask
        value = 0.5 * first.astype(jnp.float32)
        value = (value + value * jnp.tanh(value)).astype(jnp.bfloat16)
        base = (row - base_row) * VIEWS * channels
        for t in range(2):
            inner = slice(t * half, (t + 1) * half)
            if 1 <= row <= rows + 1 and chunk > 0:
                held[2 * (chunk - 1) + t, (row - base_row) * pair:(row - base_row + 1) * pair, :] = first[:, inner]
            frame = 2 * chunk + t
            act[frame, base:base + channels, :] = to_right(value[channels:, inner])
            act[frame, base + channels:base + 3 * channels, :] = value[:, inner]
            act[frame, base + 3 * channels:base + 4 * channels, :] = to_left(value[:channels, inner])


def load_kernel(pixels_hbm, first_hbm, second_hbm, down_hbm, pixels, first, second, down, chosen, columns_out, gather_own, gather_out, sems, *, rows, frames):
    arrays = ((pixels_hbm, pixels), (first_hbm, first), (second_hbm, second), (down_hbm, down))
    copies = [pltpu.make_async_copy(source, target, sems.at[i]) for i, (source, target) in enumerate(arrays)]
    for copy in copies:
        copy.start()
    colors = pixels.shape[1]
    apart, alone = act_groups(rows)
    part = (frames + 4) // HALVES

    size = TAPS**3 * SUBLANES
    line = lax.broadcasted_iota(jnp.int32, (size, 1), 0)
    tap, color = line // SUBLANES, line % SUBLANES
    target = (tap // TAPS**2 * VIEWS + tap % TAPS) * SLOT + tap // TAPS % TAPS * colors + color
    chosen[...] = one_hot(chosen.shape, target, color < colors)

    width = columns_out.shape[0]
    column = lax.broadcasted_iota(jnp.int32, columns_out.shape, 0)
    place = lax.broadcasted_iota(jnp.int32, columns_out.shape, 1)
    half = width // 2
    columns_out[...] = jnp.where(column == place % half * 2 + place // half - 1, 1.0, 0.0).astype(jnp.bfloat16)

    frame, color, row, used = band_targets(gather_own.shape[0], alone, colors)
    gather_own[...] = one_hot(gather_own.shape, (frame * colors + color) * rows + row, used)

    odd = lax.rem(lax.axis_index("frames"), 2)
    frame, color, row, used = band_targets(gather_out.shape[0], apart, colors)
    source = jnp.where(row < 0, 1 + odd, jnp.where(row < rows, 0, 2 - odd))
    local = jnp.where(row < 0, row + rows, jnp.where(row < rows, row, row - rows))
    gather_out[...] = one_hot(gather_out.shape, ((source * part + frame) * colors + color) * rows + local, used)

    for copy in copies:
        copy.wait()


def prepare_kernel(count, own, first, second, down, chosen, columns, gather, first_out, second_out, down_out, live_out, held_out, partial_out, bands, act, *, rows, frames):
    channels = first.shape[2]
    colors = first.shape[1]
    _, alone = act_groups(rows)
    half = columns.shape[1] // VIEWS

    none = jnp.zeros((channels, channels), jnp.bfloat16)
    for tap in range(TAPS * TAPS):
        taps = [second[tap * TAPS + tap_x] for tap_x in range(TAPS)]
        depths = slice(tap * VIEWS * channels, (tap + 1) * VIEWS * channels)
        second_out[:channels, depths] = jnp.concatenate(taps + [none], axis=1)
        second_out[channels:, depths] = jnp.concatenate([none] + taps, axis=1)

    part = (frames + 4) // HALVES
    size = part * colors * rows
    for number in range(HALVES):
        spread_bands(gather[...], own[number * size:(number + 1) * size, :], columns[...], bands, number * part, alone)

    frame = lax.broadcasted_iota(jnp.int32, live_out.shape, 1) // half + (lax.axis_index("frames") * frames - 2)
    row = lax.broadcasted_iota(jnp.int32, live_out.shape, 0) + (lax.axis_index("rows") * rows - 2)
    inside = jnp.logical_and(row >= 0, row < lax.axis_size("rows") * rows)
    live_out[...] = jnp.where(jnp.logical_and(inside, frame < count[0]), 1.0, 0.0)

    filler = jnp.zeros((SUBLANES - colors, channels), jnp.float32)
    lines = []
    for tap in range(TAPS**3):
        lines += [first[tap].astype(jnp.float32), filler]
    lines = jnp.concatenate(lines, axis=0).T.astype(jnp.bfloat16)
    base = jnp.dot(lines, chosen[...], preferred_element_type=jnp.float32)
    for block in range(GROUP):
        for parity in range(PARITIES):
            shift = parity * SLOT + block * colors
            moved = pltpu.roll(base, shift, 1) if shift else base
            start = (block * PARITIES + parity) * channels
            first_out[start:start + channels, :] = moved.astype(jnp.bfloat16)

    for run, (start, rows_of) in enumerate(alone):
        for chunk in range(frames // 2 + 1):
            total = first_product(first_out, bands, run, rows_of, chunk)
            activate(total, live_out, range(start, start + rows_of), chunk, act, held_out, 3, rows)

    out_rows = down_out.shape[0] // channels
    sum_rows = down_out.shape[1] // (TAPS * channels)
    taps = jnp.concatenate([down[tap] for tap in range(TAPS * TAPS)], axis=1)
    place = lax.broadcasted_iota(jnp.int32, (down_out.shape[0], channels), 0)
    channel = lax.broadcasted_iota(jnp.int32, (down_out.shape[0], channels), 1)
    total = None
    for y in range(out_rows):
        spread = (place == channel * out_rows + y).astype(jnp.float32).astype(jnp.bfloat16)
        pieces = [taps]
        before, after = 2 * y, sum_rows - TAPS - 2 * y
        if before:
            pieces = [jnp.zeros((channels, before * TAPS * channels), jnp.bfloat16)] + pieces
        if after:
            pieces = pieces + [jnp.zeros((channels, after * TAPS * channels), jnp.bfloat16)]
        part = jnp.dot(spread, jnp.concatenate(pieces, axis=1), preferred_element_type=jnp.float32)
        total = part if total is None else total + part
    down_out[...] = total.astype(jnp.bfloat16)

    for row in range(1, rows + 1):
        for chunk in range(frames // 2):
            partial_out[row - 1, chunk] = second_product(second_out, lambda line: (act, line - 3), row, chunk, tap_rows(row, rows, True))


def encode_kernel(own_ref, there_ref, back_ref, gather_ref, columns_ref, live_ref, held_own, partial_ref, first_w, second_w, down_w, out_ref, lines, bands, act, held, taps, *, rows, frames):
    half = columns_ref.shape[1] // VIEWS
    channels = second_w.shape[0] // PARITIES
    pair = PARITIES * channels
    apart, _ = act_groups(rows)
    odd = lax.rem(lax.axis_index("frames"), 2)
    row_device = lax.axis_index("rows")
    top, bottom = row_device == 0, row_device == lax.axis_size("rows") - 1
    keep_there = jnp.where(jnp.logical_or(jnp.logical_and(odd == 0, top), jnp.logical_and(odd == 1, bottom)), 0.0, 1.0).astype(jnp.bfloat16)
    keep_back = jnp.where(jnp.logical_or(jnp.logical_and(odd == 1, top), jnp.logical_and(odd == 0, bottom)), 0.0, 1.0).astype(jnp.bfloat16)
    size = own_ref.shape[0] // HALVES
    for part in range(HALVES):
        rows_of = slice(part * size, (part + 1) * size)
        base = part * 3 * size
        lines[base:base + size, :] = own_ref[rows_of, :]
        lines[base + size:base + 2 * size, :] = there_ref[rows_of, :] * keep_there
        lines[base + 2 * size:base + 3 * size, :] = back_ref[rows_of, :] * keep_back
        spread_bands(gather_ref[...], lines[base:base + 3 * size, :], columns_ref[...], bands, part * (frames + 4) // HALVES, apart)

    step = 2 * half
    chunks = frames // 2

    def second_dot(row, chunk):
        total = second_product(second_w, lambda line: (act, line), row, chunk, tap_rows(row, rows, False))
        return total + partial_ref[row - 1, chunk] if row > 0 else total

    def second_rest(row, chunk, total):
        second = total * live_ref[row + 1:row + 2, (chunk + 1) * step:(chunk + 2) * step]
        source, base = (held_own, row - 2) if 3 <= row + 1 <= rows else (held, row + 1)
        first = two_frames(source, 2 * chunk, slice(base * pair, (base + 1) * pair))
        value = (first.astype(jnp.float32) + second).astype(jnp.bfloat16)
        base = row * TAPS * channels
        for t in range(2):
            inner = slice(t * half, (t + 1) * half)
            taps[2 * chunk + t, base:base + channels, :] = to_right(value[channels:, inner])
            taps[2 * chunk + t, base + channels:base + 3 * channels, :] = value[:, inner]

    def down_conv(chunk, first_row, last_row):
        depths = slice(first_row * TAPS * channels, last_row * TAPS * channels)
        return jnp.dot(down_w[:, depths], two_frames(taps, 2 * chunk, depths), preferred_element_type=jnp.float32)

    pieces = [(run, chunk) for run in range(len(apart)) for chunk in range(chunks + 1)]
    waiting = []
    total = first_product(first_w, bands, pieces[0][0], apart[pieces[0][0]][1], pieces[0][1])
    for number, (run, chunk) in enumerate(pieces):
        beside = waiting.pop(0) if waiting else None
        parts = second_dot(*beside) if beside else None
        if number + 1 < len(pieces):
            later_run, later_chunk = pieces[number + 1]
            later = first_product(first_w, bands, later_run, apart[later_run][1], later_chunk)
        start, count = apart[run]
        activate(total, live_ref, range(start, start + count), chunk, act, held, 0, rows)
        if beside:
            second_rest(*beside, parts)
        total = later
        if chunk > 0:
            ready = [row for row in range(rows) if (row + 2 > rows) == (run > 0)]
            waiting += [(row, chunk - 1) for row in ready]
    early = None
    for row, part in waiting:
        if row == rows - 1 and early is None:
            early = [down_conv(chunk, 0, rows - 2) for chunk in range(chunks)]
        second_rest(row, part, second_dot(row, part))
    parts = [second_dot(rows, part) for part in range(chunks)]
    early = [early[chunk] + down_conv(chunk, rows - 2, rows) for chunk in range(chunks)]
    for part in range(chunks):
        second_rest(rows, part, parts[part])
    size = down_w.shape[0]
    for part in range(chunks):
        encoded = (early[part] + down_conv(part, rows, rows + 1)).astype(jnp.bfloat16)
        for t in range(2):
            frame = part * 2 + t
            out_ref[frame * size:(frame + 1) * size, :] = encoded[:, t * half:(t + 1) * half]


def hbm(array):
    return pltpu.with_memory_space_constraint(array, pltpu.HBM)


def snake(row_devices, frame_devices):
    route = []
    for left in range(0, frame_devices, 2):
        ring = [(row, left) for row in range(row_devices)] + [(row, left + 1) for row in reversed(range(row_devices))]
        ring = [row * frame_devices + frame for row, frame in ring]
        route += list(zip(ring, ring[1:] + ring[:1]))
    return route


def shards(pixels, frame_counts, weight_first, weight_second, weight_down):
    clips, frames, colors, rows, width = pixels.shape
    channels = weight_first.shape[3]
    half = width // 2
    out_rows = rows // 2
    frame_devices, row_devices = lax.axis_size("frames"), lax.axis_size("rows")
    assert clips == 1 and frames >= 4 and rows >= 3 and rows % 2 == 0 and frames % 2 == 0
    assert (GROUP + 2) * colors <= SLOT and frame_devices % 2 == 0
    bf16 = jnp.bfloat16
    frame_device = lax.axis_index("frames")
    size = frames * colors * rows
    earlier = lax.ppermute(pixels[0, -4:], "frames", [(i, (i + 1) % frame_devices) for i in range(frame_devices)])
    arrays = [
        hbm(pixels[0]),
        hbm(weight_first.transpose(0, 1, 2, 4, 3).reshape(TAPS**3, colors, channels)),
        hbm(weight_second.reshape(TAPS**3, channels, channels)),
        hbm(weight_down.reshape(TAPS**2, channels, channels)),
    ]
    apart, alone = act_groups(rows)
    part = (frames + 4) // HALVES
    lines = part * colors * rows
    shapes = [array.shape for array in arrays] + [
        (TAPS**3 * SUBLANES, TAPS * VIEWS * SLOT),
        (width, VIEWS * half),
        (part * len(alone) * SLOT, lines),
        (part * len(apart) * SLOT, 3 * lines),
    ]
    loaded, weight_first, weight_second, weight_down, chosen, columns, gather_own, gather = pl.pallas_call(
        lambda *refs: load_kernel(*refs, rows=rows, frames=frames),
        name="load",
        compiler_params=pltpu.CompilerParams(vmem_limit_bytes=8 << 20),
        in_specs=[HBM] * len(arrays),
        out_specs=[VMEM] * len(shapes),
        out_shape=[jax.ShapeDtypeStruct(shape, bf16) for shape in shapes],
        scratch_shapes=[pltpu.SemaphoreType.DMA((len(arrays),))],
    )(*arrays)
    late = loaded.reshape(size, width)
    earlier = earlier.reshape(4 * colors * rows, width)
    earlier = jnp.where(frame_device > 0, earlier, jnp.zeros_like(earlier))
    own = jnp.concatenate([earlier, late], axis=0)
    own, frame_counts = lax.optimization_barrier((own, frame_counts))
    route = snake(row_devices, frame_devices)
    axes = ("rows", "frames")
    back = lax.ppermute(own, axes, [(b, a) for a, b in route])
    there = lax.ppermute(own, axes, route)

    pair = PARITIES * channels
    wide = (frames + 2) * half
    depth = VIEWS * SLOT
    first_w, second_w, down_w, live, held_own, partial = pl.pallas_call(
        lambda *refs: prepare_kernel(*refs, rows=rows, frames=frames),
        name="prepare",
        compiler_params=pltpu.CompilerParams(vmem_limit_bytes=12 << 20),
        in_specs=[SMEM] + [VMEM] * 7,
        out_specs=[VMEM] * 6,
        out_shape=[
            jax.ShapeDtypeStruct((GROUP * pair, TAPS * depth), bf16),
            jax.ShapeDtypeStruct((pair, TAPS * TAPS * VIEWS * channels), bf16),
            jax.ShapeDtypeStruct((channels * out_rows, (rows + 1) * TAPS * channels), bf16),
            jax.ShapeDtypeStruct((rows + 3, wide), jnp.float32),
            jax.ShapeDtypeStruct((frames, (rows - 2) * pair, half), bf16),
            jax.ShapeDtypeStruct((rows, frames // 2, pair, 2 * half), jnp.float32),
        ],
        scratch_shapes=[
            pltpu.VMEM((frames + 4, len(alone) * depth, half), bf16),
            pltpu.VMEM((frames + 2, (rows - 2) * VIEWS * channels, half), bf16),
        ],
    )(frame_counts, own, weight_first, weight_second, weight_down, chosen, columns, gather_own)
    encoded = pl.pallas_call(
        lambda *refs: encode_kernel(*refs, rows=rows, frames=frames),
        name="encode",
        compiler_params=pltpu.CompilerParams(vmem_limit_bytes=24 << 20),
        in_specs=[VMEM] * 11,
        out_specs=VMEM,
        out_shape=jax.ShapeDtypeStruct((frames * channels * out_rows, half), bf16),
        scratch_shapes=[
            pltpu.VMEM((3 * own.shape[0], width), bf16),
            pltpu.VMEM((frames + 4, len(apart) * depth, half), bf16),
            pltpu.VMEM((frames + 2, (rows + 3) * VIEWS * channels, half), bf16),
            pltpu.VMEM((frames, (rows + 3) * pair, half), bf16),
            pltpu.VMEM((frames, (rows + 1) * TAPS * channels, half), bf16),
        ],
    )(own, there, back, gather, columns, live, held_own, partial, first_w, second_w, down_w)
    return encoded.reshape(1, frames, channels, out_rows, half)


def solution(mesh):
    in_specs = (
        P(("groups", "clips"), "frames", None, "rows", None),
        P(("groups", "clips")),
        P(),
        P(),
        P(),
    )
    out_specs = P(("groups", "clips"), "frames", None, "rows", None)
    return jax.shard_map(shards, mesh=mesh, in_specs=in_specs, out_specs=out_specs, check_vma=False)
```

```python
import jax
import jax.numpy as jnp
from jax import lax
from jax.experimental import pallas as pl
from jax.experimental.pallas import tpu as pltpu
from jax.sharding import PartitionSpec as P

VIEWS = 4
PARITIES = 2
TAPS = 3
GROUP = 3
SLOT = 16
SUBLANES = 8
HALVES = 2

VMEM = pl.BlockSpec(memory_space=pltpu.VMEM)
HBM = pl.BlockSpec(memory_space=pltpu.HBM)
SMEM = pl.BlockSpec(memory_space=pltpu.SMEM)


def one_hot(shape, target, valid):
    lane = lax.broadcasted_iota(jnp.int32, shape, 1)
    return jnp.where(lane == jnp.where(valid, target, -1), 1.0, 0.0).astype(jnp.bfloat16)


def act_groups(rows):
    apart = [(0, 3), (rows + 1, 2)]
    alone = [(start, min(GROUP, rows + 1 - start)) for start in range(3, rows + 1, GROUP)]
    return apart, alone


def band_targets(size, runs, colors):
    line = lax.broadcasted_iota(jnp.int32, (size, 1), 0)
    frame, run, inner = line // (len(runs) * SLOT), line // SLOT % len(runs), line % SLOT
    start, count = 0, 0
    for number, (first, rows_of) in enumerate(runs):
        start, count = jnp.where(run == number, first, start), jnp.where(run == number, rows_of + 2, count)
    return frame, inner % colors, start + inner // colors - 3, inner < count * colors


def spread_bands(gather, lines, columns, bands, first_frame, runs):
    spread = jnp.dot(gather, lines, preferred_element_type=jnp.float32).astype(jnp.bfloat16)
    spread = jnp.dot(spread, columns, preferred_element_type=jnp.float32).astype(jnp.bfloat16)
    half = bands.shape[2]
    for line in range(spread.shape[0] // SLOT):
        t, run = line // len(runs), line % len(runs)
        for view in range(VIEWS):
            place = (run * VIEWS + view) * SLOT
            bands[first_frame + t, place:place + SLOT, :] = spread[line * SLOT:(line + 1) * SLOT, view * half:(view + 1) * half]


def tap_rows(row, rows, alone):
    return [tap for tap in range(TAPS) if (3 <= row + tap <= rows) == alone]


def second_product(weights, row_source, row, chunk, row_taps):
    channels = weights.shape[0] // PARITIES
    size = VIEWS * channels
    lines, columns = [], []
    for tap_t in range(TAPS):
        for tap_y in row_taps:
            ref, line = row_source(row + tap_y)
            lines.append(two_frames(ref, 2 * chunk + tap_t, slice(line * size, (line + 1) * size)))
            start = (tap_t * TAPS + tap_y) * size
            columns.append(weights[:, start:start + size])
    return jnp.dot(jnp.concatenate(columns, axis=1), jnp.concatenate(lines, axis=0), preferred_element_type=jnp.float32)


def two_frames(ref, frame, rows_of):
    return jnp.concatenate([ref[frame, rows_of, :], ref[frame + 1, rows_of, :]], axis=1)


def to_right(value):
    lane = lax.broadcasted_iota(jnp.int32, value.shape, 1)
    return jnp.where(lane == 0, jnp.zeros_like(value), pltpu.roll(value, 1, 1))


def to_left(value):
    lane = lax.broadcasted_iota(jnp.int32, value.shape, 1)
    return jnp.where(lane == value.shape[1] - 1, jnp.zeros_like(value), pltpu.roll(value, value.shape[1] - 1, 1))


def first_product(weights, bands, run, count, chunk):
    depth = VIEWS * SLOT
    band = [two_frames(bands, 2 * chunk + tap, slice(run * depth, (run + 1) * depth)) for tap in range(TAPS)]
    pair = weights.shape[0] // GROUP
    return jnp.dot(weights[:count * pair, :], jnp.concatenate(band, axis=0), preferred_element_type=jnp.float32)


def activate(total, live, rows_of, chunk, act, held, base_row, rows):
    half = act.shape[2]
    pair = total.shape[0] // len(rows_of)
    channels = pair // PARITIES
    for block, row in enumerate(rows_of):
        mask = live[row:row + 1, 2 * chunk * half:2 * (chunk + 1) * half].astype(jnp.bfloat16)
        first = total[block * pair:(block + 1) * pair, :].astype(jnp.bfloat16) * mask
        value = first.astype(jnp.float32)
        value = (value + value * jnp.tanh(value)).astype(jnp.bfloat16)
        base = (row - base_row) * VIEWS * channels
        for t in range(2):
            inner = slice(t * half, (t + 1) * half)
            if 1 <= row <= rows + 1 and chunk > 0:
                held[2 * (chunk - 1) + t, (row - base_row) * pair:(row - base_row + 1) * pair, :] = first[:, inner]
            frame = 2 * chunk + t
            act[frame, base:base + channels, :] = to_right(value[channels:, inner])
            act[frame, base + channels:base + 3 * channels, :] = value[:, inner]
            act[frame, base + 3 * channels:base + 4 * channels, :] = to_left(value[:channels, inner])


def load_kernel(pixels_hbm, first_hbm, second_hbm, down_hbm, pixels, first, second, down, chosen, columns_out, gather_own, gather_out, sems, *, rows, frames):
    arrays = ((pixels_hbm, pixels), (first_hbm, first), (second_hbm, second), (down_hbm, down))
    copies = [pltpu.make_async_copy(source, target, sems.at[i]) for i, (source, target) in enumerate(arrays)]
    for copy in copies:
        copy.start()
    colors = pixels.shape[1]
    apart, alone = act_groups(rows)
    part = (frames + 4) // HALVES

    size = TAPS**3 * SUBLANES
    line = lax.broadcasted_iota(jnp.int32, (size, 1), 0)
    tap, color = line // SUBLANES, line % SUBLANES
    target = (tap // TAPS**2 * VIEWS + tap % TAPS) * SLOT + tap // TAPS % TAPS * colors + color
    chosen[...] = one_hot(chosen.shape, target, color < colors)

    width = columns_out.shape[0]
    column = lax.broadcasted_iota(jnp.int32, columns_out.shape, 0)
    place = lax.broadcasted_iota(jnp.int32, columns_out.shape, 1)
    half = width // 2
    columns_out[...] = jnp.where(column == place % half * 2 + place // half - 1, 1.0, 0.0).astype(jnp.bfloat16)

    frame, color, row, used = band_targets(gather_own.shape[0], alone, colors)
    gather_own[...] = one_hot(gather_own.shape, (frame * colors + color) * rows + row, used)

    odd = lax.rem(lax.axis_index("frames"), 2)
    frame, color, row, used = band_targets(gather_out.shape[0], apart, colors)
    source = jnp.where(row < 0, 1 + odd, jnp.where(row < rows, 0, 2 - odd))
    local = jnp.where(row < 0, row + rows, jnp.where(row < rows, row, row - rows))
    gather_out[...] = one_hot(gather_out.shape, ((source * part + frame) * colors + color) * rows + local, used)

    for copy in copies:
        copy.wait()


def prepare_kernel(count, own, first, second, down, chosen, columns, gather, first_out, second_out, down_out, live_out, held_out, partial_out, bands, act, *, rows, frames):
    channels = first.shape[2]
    colors = first.shape[1]
    _, alone = act_groups(rows)
    half = columns.shape[1] // VIEWS

    none = jnp.zeros((channels, channels), jnp.bfloat16)
    for tap in range(TAPS * TAPS):
        taps = [second[tap * TAPS + tap_x] for tap_x in range(TAPS)]
        depths = slice(tap * VIEWS * channels, (tap + 1) * VIEWS * channels)
        second_out[:channels, depths] = jnp.concatenate(taps + [none], axis=1)
        second_out[channels:, depths] = jnp.concatenate([none] + taps, axis=1)

    part = (frames + 4) // HALVES
    size = part * colors * rows
    for number in range(HALVES):
        spread_bands(gather[...], own[number * size:(number + 1) * size, :], columns[...], bands, number * part, alone)

    frame = lax.broadcasted_iota(jnp.int32, live_out.shape, 1) // half + (lax.axis_index("frames") * frames - 2)
    row = lax.broadcasted_iota(jnp.int32, live_out.shape, 0) + (lax.axis_index("rows") * rows - 2)
    inside = jnp.logical_and(row >= 0, row < lax.axis_size("rows") * rows)
    live_out[...] = jnp.where(jnp.logical_and(inside, frame < count[0]), 1.0, 0.0)

    filler = jnp.zeros((SUBLANES - colors, channels), jnp.float32)
    lines = []
    for tap in range(TAPS**3):
        lines += [first[tap].astype(jnp.float32), filler]
    lines = jnp.concatenate(lines, axis=0).T.astype(jnp.bfloat16)
    base = 0.5 * jnp.dot(lines, chosen[...], preferred_element_type=jnp.float32)
    for block in range(GROUP):
        for parity in range(PARITIES):
            shift = parity * SLOT + block * colors
            moved = pltpu.roll(base, shift, 1) if shift else base
            start = (block * PARITIES + parity) * channels
            first_out[start:start + channels, :] = moved.astype(jnp.bfloat16)

    for run, (start, rows_of) in enumerate(alone):
        for chunk in range(frames // 2 + 1):
            total = first_product(first_out, bands, run, rows_of, chunk)
            activate(total, live_out, range(start, start + rows_of), chunk, act, held_out, 3, rows)

    out_rows = down_out.shape[0] // channels
    sum_rows = down_out.shape[1] // (TAPS * channels)
    taps = jnp.concatenate([down[tap] for tap in range(TAPS * TAPS)], axis=1)
    place = lax.broadcasted_iota(jnp.int32, (down_out.shape[0], channels), 0)
    channel = lax.broadcasted_iota(jnp.int32, (down_out.shape[0], channels), 1)
    total = None
    for y in range(out_rows):
        spread = (place == channel * out_rows + y).astype(jnp.float32).astype(jnp.bfloat16)
        pieces = [taps]
        before, after = 2 * y, sum_rows - TAPS - 2 * y
        if before:
            pieces = [jnp.zeros((channels, before * TAPS * channels), jnp.bfloat16)] + pieces
        if after:
            pieces = pieces + [jnp.zeros((channels, after * TAPS * channels), jnp.bfloat16)]
        part = jnp.dot(spread, jnp.concatenate(pieces, axis=1), preferred_element_type=jnp.float32)
        total = part if total is None else total + part
    down_out[...] = total.astype(jnp.bfloat16)

    for row in range(1, rows + 1):
        for chunk in range(frames // 2):
            partial_out[row - 1, chunk] = second_product(second_out, lambda line: (act, line - 3), row, chunk, tap_rows(row, rows, True))


def encode_kernel(own_ref, there_ref, back_ref, gather_ref, columns_ref, live_ref, held_own, partial_ref, first_w, second_w, down_w, out_ref, lines, bands, act, held, taps, *, rows, frames):
    half = columns_ref.shape[1] // VIEWS
    channels = second_w.shape[0] // PARITIES
    pair = PARITIES * channels
    apart, _ = act_groups(rows)
    odd = lax.rem(lax.axis_index("frames"), 2)
    row_device = lax.axis_index("rows")
    top, bottom = row_device == 0, row_device == lax.axis_size("rows") - 1
    keep_there = jnp.where(jnp.logical_or(jnp.logical_and(odd == 0, top), jnp.logical_and(odd == 1, bottom)), 0.0, 1.0).astype(jnp.bfloat16)
    keep_back = jnp.where(jnp.logical_or(jnp.logical_and(odd == 1, top), jnp.logical_and(odd == 0, bottom)), 0.0, 1.0).astype(jnp.bfloat16)
    size = own_ref.shape[0] // HALVES
    for part in range(HALVES):
        rows_of = slice(part * size, (part + 1) * size)
        base = part * 3 * size
        lines[base:base + size, :] = own_ref[rows_of, :]
        lines[base + size:base + 2 * size, :] = there_ref[rows_of, :] * keep_there
        lines[base + 2 * size:base + 3 * size, :] = back_ref[rows_of, :] * keep_back
        spread_bands(gather_ref[...], lines[base:base + 3 * size, :], columns_ref[...], bands, part * (frames + 4) // HALVES, apart)

    step = 2 * half
    chunks = frames // 2

    def second_dot(row, chunk):
        total = second_product(second_w, lambda line: (act, line), row, chunk, tap_rows(row, rows, False))
        return total + partial_ref[row - 1, chunk] if row > 0 else total

    def second_rest(row, chunk, total):
        second = total * live_ref[row + 1:row + 2, (chunk + 1) * step:(chunk + 2) * step]
        source, base = (held_own, row - 2) if 3 <= row + 1 <= rows else (held, row + 1)
        first = two_frames(source, 2 * chunk, slice(base * pair, (base + 1) * pair))
        value = (2 * first.astype(jnp.float32) + second).astype(jnp.bfloat16)
        base = row * TAPS * channels
        for t in range(2):
            inner = slice(t * half, (t + 1) * half)
            taps[2 * chunk + t, base:base + channels, :] = to_right(value[channels:, inner])
            taps[2 * chunk + t, base + channels:base + 3 * channels, :] = value[:, inner]

    def down_conv(chunk, first_row, last_row):
        depths = slice(first_row * TAPS * channels, last_row * TAPS * channels)
        return jnp.dot(down_w[:, depths], two_frames(taps, 2 * chunk, depths), preferred_element_type=jnp.float32)

    pieces = [(run, chunk) for run in range(len(apart)) for chunk in range(chunks + 1)]
    waiting = []
    total = first_product(first_w, bands, pieces[0][0], apart[pieces[0][0]][1], pieces[0][1])
    for number, (run, chunk) in enumerate(pieces):
        beside = waiting.pop(0) if waiting else None
        parts = second_dot(*beside) if beside else None
        if number + 1 < len(pieces):
            later_run, later_chunk = pieces[number + 1]
            later = first_product(first_w, bands, later_run, apart[later_run][1], later_chunk)
        start, count = apart[run]
        activate(total, live_ref, range(start, start + count), chunk, act, held, 0, rows)
        if beside:
            second_rest(*beside, parts)
        total = later
        if chunk > 0:
            ready = [row for row in range(rows) if (row + 2 > rows) == (run > 0)]
            waiting += [(row, chunk - 1) for row in ready]
    early = None
    for row, part in waiting:
        if row == rows - 1 and early is None:
            early = [down_conv(chunk, 0, rows - 2) for chunk in range(chunks)]
        second_rest(row, part, second_dot(row, part))
    parts = [second_dot(rows, part) for part in range(chunks)]
    early = [early[chunk] + down_conv(chunk, rows - 2, rows) for chunk in range(chunks)]
    for part in range(chunks):
        second_rest(rows, part, parts[part])
    size = down_w.shape[0]
    for part in range(chunks):
        encoded = (early[part] + down_conv(part, rows, rows + 1)).astype(jnp.bfloat16)
        for t in range(2):
            frame = part * 2 + t
            out_ref[frame * size:(frame + 1) * size, :] = encoded[:, t * half:(t + 1) * half]


def hbm(array):
    return pltpu.with_memory_space_constraint(array, pltpu.HBM)


def snake(row_devices, frame_devices):
    route = []
    for left in range(0, frame_devices, 2):
        ring = [(row, left) for row in range(row_devices)] + [(row, left + 1) for row in reversed(range(row_devices))]
        ring = [row * frame_devices + frame for row, frame in ring]
        route += list(zip(ring, ring[1:] + ring[:1]))
    return route


def shards(pixels, frame_counts, weight_first, weight_second, weight_down):
    clips, frames, colors, rows, width = pixels.shape
    channels = weight_first.shape[3]
    half = width // 2
    out_rows = rows // 2
    frame_devices, row_devices = lax.axis_size("frames"), lax.axis_size("rows")
    assert clips == 1 and frames >= 4 and rows >= 3 and rows % 2 == 0 and frames % 2 == 0
    assert (GROUP + 2) * colors <= SLOT and frame_devices % 2 == 0
    bf16 = jnp.bfloat16
    frame_device = lax.axis_index("frames")
    size = frames * colors * rows
    earlier = lax.ppermute(pixels[0, -4:], "frames", [(i, (i + 1) % frame_devices) for i in range(frame_devices)])
    arrays = [
        hbm(pixels[0]),
        hbm(weight_first.transpose(0, 1, 2, 4, 3).reshape(TAPS**3, colors, channels)),
        hbm(weight_second.reshape(TAPS**3, channels, channels)),
        hbm(weight_down.reshape(TAPS**2, channels, channels)),
    ]
    apart, alone = act_groups(rows)
    part = (frames + 4) // HALVES
    lines = part * colors * rows
    shapes = [array.shape for array in arrays] + [
        (TAPS**3 * SUBLANES, TAPS * VIEWS * SLOT),
        (width, VIEWS * half),
        (part * len(alone) * SLOT, lines),
        (part * len(apart) * SLOT, 3 * lines),
    ]
    loaded, weight_first, weight_second, weight_down, chosen, columns, gather_own, gather = pl.pallas_call(
        lambda *refs: load_kernel(*refs, rows=rows, frames=frames),
        name="load",
        compiler_params=pltpu.CompilerParams(vmem_limit_bytes=8 << 20),
        in_specs=[HBM] * len(arrays),
        out_specs=[VMEM] * len(shapes),
        out_shape=[jax.ShapeDtypeStruct(shape, bf16) for shape in shapes],
        scratch_shapes=[pltpu.SemaphoreType.DMA((len(arrays),))],
    )(*arrays)
    late = loaded.reshape(size, width)
    earlier = earlier.reshape(4 * colors * rows, width)
    earlier = jnp.where(frame_device > 0, earlier, jnp.zeros_like(earlier))
    own = jnp.concatenate([earlier, late], axis=0)
    own, frame_counts = lax.optimization_barrier((own, frame_counts))
    route = snake(row_devices, frame_devices)
    axes = ("rows", "frames")
    back = lax.ppermute(own, axes, [(b, a) for a, b in route])
    there = lax.ppermute(own, axes, route)

    pair = PARITIES * channels
    wide = (frames + 2) * half
    depth = VIEWS * SLOT
    first_w, second_w, down_w, live, held_own, partial = pl.pallas_call(
        lambda *refs: prepare_kernel(*refs, rows=rows, frames=frames),
        name="prepare",
        compiler_params=pltpu.CompilerParams(vmem_limit_bytes=12 << 20),
        in_specs=[SMEM] + [VMEM] * 7,
        out_specs=[VMEM] * 6,
        out_shape=[
            jax.ShapeDtypeStruct((GROUP * pair, TAPS * depth), bf16),
            jax.ShapeDtypeStruct((pair, TAPS * TAPS * VIEWS * channels), bf16),
            jax.ShapeDtypeStruct((channels * out_rows, (rows + 1) * TAPS * channels), bf16),
            jax.ShapeDtypeStruct((rows + 3, wide), jnp.float32),
            jax.ShapeDtypeStruct((frames, (rows - 2) * pair, half), bf16),
            jax.ShapeDtypeStruct((rows, frames // 2, pair, 2 * half), jnp.float32),
        ],
        scratch_shapes=[
            pltpu.VMEM((frames + 4, len(alone) * depth, half), bf16),
            pltpu.VMEM((frames + 2, (rows - 2) * VIEWS * channels, half), bf16),
        ],
    )(frame_counts, own, weight_first, weight_second, weight_down, chosen, columns, gather_own)
    encoded = pl.pallas_call(
        lambda *refs: encode_kernel(*refs, rows=rows, frames=frames),
        name="encode",
        compiler_params=pltpu.CompilerParams(vmem_limit_bytes=24 << 20),
        in_specs=[VMEM] * 11,
        out_specs=VMEM,
        out_shape=jax.ShapeDtypeStruct((frames * channels * out_rows, half), bf16),
        scratch_shapes=[
            pltpu.VMEM((3 * own.shape[0], width), bf16),
            pltpu.VMEM((frames + 4, len(apart) * depth, half), bf16),
            pltpu.VMEM((frames + 2, (rows + 3) * VIEWS * channels, half), bf16),
            pltpu.VMEM((frames, (rows + 3) * pair, half), bf16),
            pltpu.VMEM((frames, (rows + 1) * TAPS * channels, half), bf16),
        ],
    )(own, there, back, gather, columns, live, held_own, partial, first_w, second_w, down_w)
    return encoded.reshape(1, frames, channels, out_rows, half)


def solution(mesh):
    in_specs = (
        P(("groups", "clips"), "frames", None, "rows", None),
        P(("groups", "clips")),
        P(),
        P(),
        P(),
    )
    out_specs = P(("groups", "clips"), "frames", None, "rows", None)
    return jax.shard_map(shards, mesh=mesh, in_specs=in_specs, out_specs=out_specs, check_vma=False)
```

```python
import jax
import jax.numpy as jnp
from jax import lax
from jax.experimental import pallas as pl
from jax.experimental.pallas import tpu as pltpu
from jax.sharding import PartitionSpec as P

VIEWS = 4
PARITIES = 2
TAPS = 3
GROUP = 3
SLOT = 16
SUBLANES = 8
HALVES = 2

VMEM = pl.BlockSpec(memory_space=pltpu.VMEM)
HBM = pl.BlockSpec(memory_space=pltpu.HBM)
SMEM = pl.BlockSpec(memory_space=pltpu.SMEM)


def one_hot(shape, target, valid):
    lane = lax.broadcasted_iota(jnp.int32, shape, 1)
    return jnp.where(lane == jnp.where(valid, target, -1), 1.0, 0.0).astype(jnp.bfloat16)


def act_groups(rows):
    apart = [(0, 3), (rows + 1, 2)]
    alone = [(start, min(GROUP, rows + 1 - start)) for start in range(3, rows + 1, GROUP)]
    return apart, alone


def band_targets(size, runs, colors):
    line = lax.broadcasted_iota(jnp.int32, (size, 1), 0)
    frame, run, inner = line // (len(runs) * SLOT), line // SLOT % len(runs), line % SLOT
    start, count = 0, 0
    for number, (first, rows_of) in enumerate(runs):
        start, count = jnp.where(run == number, first, start), jnp.where(run == number, rows_of + 2, count)
    return frame, inner % colors, start + inner // colors - 3, inner < count * colors


def spread_bands(gather, lines, columns, bands, first_frame, runs):
    spread = jnp.dot(gather, lines, preferred_element_type=jnp.float32).astype(jnp.bfloat16)
    spread = jnp.dot(spread, columns, preferred_element_type=jnp.float32).astype(jnp.bfloat16)
    half = bands.shape[2]
    for line in range(spread.shape[0] // SLOT):
        t, run = line // len(runs), line % len(runs)
        for view in range(VIEWS):
            place = (run * VIEWS + view) * SLOT
            bands[first_frame + t, place:place + SLOT, :] = spread[line * SLOT:(line + 1) * SLOT, view * half:(view + 1) * half]


def tap_rows(row, rows, alone):
    return [tap for tap in range(TAPS) if (3 <= row + tap <= rows) == alone]


def second_product(weights, row_source, row, chunk, row_taps):
    channels = weights.shape[0] // PARITIES
    size = VIEWS * channels
    lines, columns = [], []
    for tap_t in range(TAPS):
        for tap_y in row_taps:
            ref, line = row_source(row + tap_y)
            lines.append(two_frames(ref, 2 * chunk + tap_t, slice(line * size, (line + 1) * size)))
            start = (tap_t * TAPS + tap_y) * size
            columns.append(weights[:, start:start + size])
    return jnp.dot(jnp.concatenate(columns, axis=1), jnp.concatenate(lines, axis=0), preferred_element_type=jnp.float32)


def two_frames(ref, frame, rows_of):
    return jnp.concatenate([ref[frame, rows_of, :], ref[frame + 1, rows_of, :]], axis=1)


def to_right(value):
    lane = lax.broadcasted_iota(jnp.int32, value.shape, 1)
    return jnp.where(lane == 0, jnp.zeros_like(value), pltpu.roll(value, 1, 1))


def to_left(value):
    lane = lax.broadcasted_iota(jnp.int32, value.shape, 1)
    return jnp.where(lane == value.shape[1] - 1, jnp.zeros_like(value), pltpu.roll(value, value.shape[1] - 1, 1))


def first_product(weights, bands, run, count, chunk):
    depth = VIEWS * SLOT
    band = [two_frames(bands, 2 * chunk + tap, slice(run * depth, (run + 1) * depth)) for tap in range(TAPS)]
    pair = weights.shape[0] // GROUP
    return jnp.dot(weights[:count * pair, :], jnp.concatenate(band, axis=0), preferred_element_type=jnp.float32)


def activate(total, live, rows_of, chunk, act, held, base_row, rows):
    half = act.shape[2]
    pair = total.shape[0] // len(rows_of)
    channels = pair // PARITIES
    for block, row in enumerate(rows_of):
        mask = live[row:row + 1, 2 * chunk * half:2 * (chunk + 1) * half].astype(jnp.bfloat16)
        first = total[block * pair:(block + 1) * pair, :].astype(jnp.bfloat16) * mask
        value = 0.5 * first.astype(jnp.float32)
        value = (value + value * jnp.tanh(value)).astype(jnp.bfloat16)
        base = (row - base_row) * VIEWS * channels
        for t in range(2):
            inner = slice(t * half, (t + 1) * half)
            if 1 <= row <= rows + 1 and chunk > 0:
                held[2 * (chunk - 1) + t, (row - base_row) * pair:(row - base_row + 1) * pair, :] = first[:, inner]
            frame = 2 * chunk + t
            act[frame, base:base + channels, :] = to_right(value[channels:, inner])
            act[frame, base + channels:base + 3 * channels, :] = value[:, inner]
            act[frame, base + 3 * channels:base + 4 * channels, :] = to_left(value[:channels, inner])


def load_kernel(pixels_hbm, first_hbm, second_hbm, down_hbm, pixels, first, second, down, chosen, columns_out, gather_own, gather_out, sems, *, rows, frames):
    arrays = ((pixels_hbm, pixels), (first_hbm, first), (second_hbm, second), (down_hbm, down))
    copies = [pltpu.make_async_copy(source, target, sems.at[i]) for i, (source, target) in enumerate(arrays)]
    for copy in copies:
        copy.start()
    colors = pixels.shape[1]
    apart, alone = act_groups(rows)
    part = (frames + 4) // HALVES

    size = TAPS**3 * SUBLANES
    line = lax.broadcasted_iota(jnp.int32, (size, 1), 0)
    tap, color = line // SUBLANES, line % SUBLANES
    target = (tap // TAPS**2 * VIEWS + tap % TAPS) * SLOT + tap // TAPS % TAPS * colors + color
    chosen[...] = one_hot(chosen.shape, target, color < colors)

    width = columns_out.shape[0]
    column = lax.broadcasted_iota(jnp.int32, columns_out.shape, 0)
    place = lax.broadcasted_iota(jnp.int32, columns_out.shape, 1)
    half = width // 2
    columns_out[...] = jnp.where(column == place % half * 2 + place // half - 1, 1.0, 0.0).astype(jnp.bfloat16)

    frame, color, row, used = band_targets(gather_own.shape[0], alone, colors)
    gather_own[...] = one_hot(gather_own.shape, (frame * colors + color) * rows + row, used)

    odd = lax.rem(lax.axis_index("frames"), 2)
    frame, color, row, used = band_targets(gather_out.shape[0], apart, colors)
    source = jnp.where(row < 0, 1 + odd, jnp.where(row < rows, 0, 2 - odd))
    local = jnp.where(row < 0, row + rows, jnp.where(row < rows, row, row - rows))
    gather_out[...] = one_hot(gather_out.shape, ((source * part + frame) * colors + color) * rows + local, used)

    for copy in copies:
        copy.wait()


def prepare_kernel(count, own, first, second, down, chosen, columns, gather, first_out, second_out, down_out, live_out, held_out, partial_out, bands, act, *, rows, frames):
    channels = first.shape[2]
    colors = first.shape[1]
    _, alone = act_groups(rows)
    half = columns.shape[1] // VIEWS

    none = jnp.zeros((channels, channels), jnp.bfloat16)
    for tap in range(TAPS * TAPS):
        taps = [second[tap * TAPS + tap_x] for tap_x in range(TAPS)]
        depths = slice(tap * VIEWS * channels, (tap + 1) * VIEWS * channels)
        second_out[:channels, depths] = jnp.concatenate(taps + [none], axis=1)
        second_out[channels:, depths] = jnp.concatenate([none] + taps, axis=1)

    part = (frames + 4) // HALVES
    size = part * colors * rows
    for number in range(HALVES):
        spread_bands(gather[...], own[number * size:(number + 1) * size, :], columns[...], bands, number * part, alone)

    frame = lax.broadcasted_iota(jnp.int32, live_out.shape, 1) // half + (lax.axis_index("frames") * frames - 2)
    row = lax.broadcasted_iota(jnp.int32, live_out.shape, 0) + (lax.axis_index("rows") * rows - 2)
    inside = jnp.logical_and(row >= 0, row < lax.axis_size("rows") * rows)
    live_out[...] = jnp.where(jnp.logical_and(inside, frame < count[0]), 1.0, 0.0)

    filler = jnp.zeros((SUBLANES - colors, channels), jnp.float32)
    lines = []
    for tap in range(TAPS**3):
        lines += [first[tap].astype(jnp.float32), filler]
    lines = jnp.concatenate(lines, axis=0).T.astype(jnp.bfloat16)
    base = jnp.dot(lines, chosen[...], preferred_element_type=jnp.float32)
    for block in range(GROUP):
        for parity in range(PARITIES):
            shift = parity * SLOT + block * colors
            moved = pltpu.roll(base, shift, 1) if shift else base
            start = (block * PARITIES + parity) * channels
            first_out[start:start + channels, :] = moved.astype(jnp.bfloat16)

    for run, (start, rows_of) in enumerate(alone):
        totals = [first_product(first_out, bands, run, rows_of, chunk) for chunk in range(frames // 2 + 1)]
        for chunk, total in enumerate(totals):
            activate(total, live_out, range(start, start + rows_of), chunk, act, held_out, 3, rows)

    out_rows = down_out.shape[0] // channels
    sum_rows = down_out.shape[1] // (TAPS * channels)
    taps = jnp.concatenate([down[tap] for tap in range(TAPS * TAPS)], axis=1)
    place = lax.broadcasted_iota(jnp.int32, (down_out.shape[0], channels), 0)
    channel = lax.broadcasted_iota(jnp.int32, (down_out.shape[0], channels), 1)
    total = None
    for y in range(out_rows):
        spread = (place == channel * out_rows + y).astype(jnp.float32).astype(jnp.bfloat16)
        pieces = [taps]
        before, after = 2 * y, sum_rows - TAPS - 2 * y
        if before:
            pieces = [jnp.zeros((channels, before * TAPS * channels), jnp.bfloat16)] + pieces
        if after:
            pieces = pieces + [jnp.zeros((channels, after * TAPS * channels), jnp.bfloat16)]
        part = jnp.dot(spread, jnp.concatenate(pieces, axis=1), preferred_element_type=jnp.float32)
        total = part if total is None else total + part
    down_out[...] = total.astype(jnp.bfloat16)

    for row in range(1, rows + 1):
        for chunk in range(frames // 2):
            partial_out[row - 1, chunk] = second_product(second_out, lambda line: (act, line - 3), row, chunk, tap_rows(row, rows, True))


def encode_kernel(own_ref, there_ref, back_ref, gather_ref, columns_ref, live_ref, held_own, partial_ref, first_w, second_w, down_w, out_ref, bands, act, held, taps, *, rows, frames):
    half = columns_ref.shape[1] // VIEWS
    channels = second_w.shape[0] // PARITIES
    pair = PARITIES * channels
    apart, _ = act_groups(rows)
    odd = lax.rem(lax.axis_index("frames"), 2)
    row_device = lax.axis_index("rows")
    top, bottom = row_device == 0, row_device == lax.axis_size("rows") - 1
    keep_there = jnp.where(jnp.logical_or(jnp.logical_and(odd == 0, top), jnp.logical_and(odd == 1, bottom)), 0.0, 1.0).astype(jnp.bfloat16)
    keep_back = jnp.where(jnp.logical_or(jnp.logical_and(odd == 1, top), jnp.logical_and(odd == 0, bottom)), 0.0, 1.0).astype(jnp.bfloat16)
    size = own_ref.shape[0] // HALVES
    for part in range(HALVES):
        rows_of = slice(part * size, (part + 1) * size)
        lines = jnp.concatenate([own_ref[rows_of, :], there_ref[rows_of, :] * keep_there, back_ref[rows_of, :] * keep_back], axis=0)
        spread_bands(gather_ref[...], lines, columns_ref[...], bands, part * (frames + 4) // HALVES, apart)

    step = 2 * half
    chunks = frames // 2

    def second_dot(row, chunk):
        total = second_product(second_w, lambda line: (act, line), row, chunk, tap_rows(row, rows, False))
        return total + partial_ref[row - 1, chunk] if row > 0 else total

    def second_rest(row, chunk, total):
        second = total * live_ref[row + 1:row + 2, (chunk + 1) * step:(chunk + 2) * step]
        source, base = (held_own, row - 2) if 3 <= row + 1 <= rows else (held, row + 1)
        first = two_frames(source, 2 * chunk, slice(base * pair, (base + 1) * pair))
        value = (first.astype(jnp.float32) + second).astype(jnp.bfloat16)
        base = row * TAPS * channels
        for t in range(2):
            inner = slice(t * half, (t + 1) * half)
            taps[2 * chunk + t, base:base + channels, :] = to_right(value[channels:, inner])
            taps[2 * chunk + t, base + channels:base + 3 * channels, :] = value[:, inner]

    def down_conv(chunk, first_row, last_row):
        depths = slice(first_row * TAPS * channels, last_row * TAPS * channels)
        return jnp.dot(down_w[:, depths], two_frames(taps, 2 * chunk, depths), preferred_element_type=jnp.float32)

    pieces = [(run, chunk) for run in range(len(apart)) for chunk in range(chunks + 1)]
    waiting = []
    total = first_product(first_w, bands, pieces[0][0], apart[pieces[0][0]][1], pieces[0][1])
    for number, (run, chunk) in enumerate(pieces):
        beside = waiting.pop(0) if waiting else None
        parts = second_dot(*beside) if beside else None
        if number + 1 < len(pieces):
            later_run, later_chunk = pieces[number + 1]
            later = first_product(first_w, bands, later_run, apart[later_run][1], later_chunk)
        start, count = apart[run]
        activate(total, live_ref, range(start, start + count), chunk, act, held, 0, rows)
        if beside:
            second_rest(*beside, parts)
        total = later
        if chunk > 0:
            ready = [row for row in range(rows) if (row + 2 > rows) == (run > 0)]
            waiting += [(row, chunk - 1) for row in ready]
    early = None
    for row, part in waiting:
        if row == rows - 1 and early is None:
            early = [down_conv(chunk, 0, rows - 2) for chunk in range(chunks)]
        second_rest(row, part, second_dot(row, part))
    parts = [second_dot(rows, part) for part in range(chunks)]
    early = [early[chunk] + down_conv(chunk, rows - 2, rows) for chunk in range(chunks)]
    for part in range(chunks):
        second_rest(rows, part, parts[part])
    size = down_w.shape[0]
    for part in range(chunks):
        encoded = (early[part] + down_conv(part, rows, rows + 1)).astype(jnp.bfloat16)
        for t in range(2):
            frame = part * 2 + t
            out_ref[frame * size:(frame + 1) * size, :] = encoded[:, t * half:(t + 1) * half]


def hbm(array):
    return pltpu.with_memory_space_constraint(array, pltpu.HBM)


def snake(row_devices, frame_devices):
    route = []
    for left in range(0, frame_devices, 2):
        ring = [(row, left) for row in range(row_devices)] + [(row, left + 1) for row in reversed(range(row_devices))]
        ring = [row * frame_devices + frame for row, frame in ring]
        route += list(zip(ring, ring[1:] + ring[:1]))
    return route


def shards(pixels, frame_counts, weight_first, weight_second, weight_down):
    clips, frames, colors, rows, width = pixels.shape
    channels = weight_first.shape[3]
    half = width // 2
    out_rows = rows // 2
    frame_devices, row_devices = lax.axis_size("frames"), lax.axis_size("rows")
    assert clips == 1 and frames >= 4 and rows >= 3 and rows % 2 == 0 and frames % 2 == 0
    assert (GROUP + 2) * colors <= SLOT and frame_devices % 2 == 0
    bf16 = jnp.bfloat16
    frame_device = lax.axis_index("frames")
    size = frames * colors * rows
    earlier = lax.ppermute(pixels[0, -4:], "frames", [(i, (i + 1) % frame_devices) for i in range(frame_devices)])
    arrays = [
        hbm(pixels[0]),
        hbm(weight_first.transpose(0, 1, 2, 4, 3).reshape(TAPS**3, colors, channels)),
        hbm(weight_second.reshape(TAPS**3, channels, channels)),
        hbm(weight_down.reshape(TAPS**2, channels, channels)),
    ]
    apart, alone = act_groups(rows)
    part = (frames + 4) // HALVES
    lines = part * colors * rows
    shapes = [array.shape for array in arrays] + [
        (TAPS**3 * SUBLANES, TAPS * VIEWS * SLOT),
        (width, VIEWS * half),
        (part * len(alone) * SLOT, lines),
        (part * len(apart) * SLOT, 3 * lines),
    ]
    loaded, weight_first, weight_second, weight_down, chosen, columns, gather_own, gather = pl.pallas_call(
        lambda *refs: load_kernel(*refs, rows=rows, frames=frames),
        name="load",
        compiler_params=pltpu.CompilerParams(vmem_limit_bytes=8 << 20),
        in_specs=[HBM] * len(arrays),
        out_specs=[VMEM] * len(shapes),
        out_shape=[jax.ShapeDtypeStruct(shape, bf16) for shape in shapes],
        scratch_shapes=[pltpu.SemaphoreType.DMA((len(arrays),))],
    )(*arrays)
    late = loaded.reshape(size, width)
    earlier = earlier.reshape(4 * colors * rows, width)
    earlier = jnp.where(frame_device > 0, earlier, jnp.zeros_like(earlier))
    own = jnp.concatenate([earlier, late], axis=0)
    own, frame_counts = lax.optimization_barrier((own, frame_counts))
    route = snake(row_devices, frame_devices)
    axes = ("rows", "frames")
    back = lax.ppermute(own, axes, [(b, a) for a, b in route])
    there = lax.ppermute(own, axes, route)

    pair = PARITIES * channels
    wide = (frames + 2) * half
    depth = VIEWS * SLOT
    first_w, second_w, down_w, live, held_own, partial = pl.pallas_call(
        lambda *refs: prepare_kernel(*refs, rows=rows, frames=frames),
        name="prepare",
        compiler_params=pltpu.CompilerParams(vmem_limit_bytes=12 << 20),
        in_specs=[SMEM] + [VMEM] * 7,
        out_specs=[VMEM] * 6,
        out_shape=[
            jax.ShapeDtypeStruct((GROUP * pair, TAPS * depth), bf16),
            jax.ShapeDtypeStruct((pair, TAPS * TAPS * VIEWS * channels), bf16),
            jax.ShapeDtypeStruct((channels * out_rows, (rows + 1) * TAPS * channels), bf16),
            jax.ShapeDtypeStruct((rows + 3, wide), jnp.float32),
            jax.ShapeDtypeStruct((frames, (rows - 2) * pair, half), bf16),
            jax.ShapeDtypeStruct((rows, frames // 2, pair, 2 * half), jnp.float32),
        ],
        scratch_shapes=[
            pltpu.VMEM((frames + 4, len(alone) * depth, half), bf16),
            pltpu.VMEM((frames + 2, (rows - 2) * VIEWS * channels, half), bf16),
        ],
    )(frame_counts, own, weight_first, weight_second, weight_down, chosen, columns, gather_own)
    encoded = pl.pallas_call(
        lambda *refs: encode_kernel(*refs, rows=rows, frames=frames),
        name="encode",
        compiler_params=pltpu.CompilerParams(vmem_limit_bytes=24 << 20),
        in_specs=[VMEM] * 11,
        out_specs=VMEM,
        out_shape=jax.ShapeDtypeStruct((frames * channels * out_rows, half), bf16),
        scratch_shapes=[
            pltpu.VMEM((frames + 4, len(apart) * depth, half), bf16),
            pltpu.VMEM((frames + 2, (rows + 3) * VIEWS * channels, half), bf16),
            pltpu.VMEM((frames, (rows + 3) * pair, half), bf16),
            pltpu.VMEM((frames, (rows + 1) * TAPS * channels, half), bf16),
        ],
    )(own, there, back, gather, columns, live, held_own, partial, first_w, second_w, down_w)
    return encoded.reshape(1, frames, channels, out_rows, half)


def solution(mesh):
    in_specs = (
        P(("groups", "clips"), "frames", None, "rows", None),
        P(("groups", "clips")),
        P(),
        P(),
        P(),
    )
    out_specs = P(("groups", "clips"), "frames", None, "rows", None)
    return jax.shard_map(shards, mesh=mesh, in_specs=in_specs, out_specs=out_specs, check_vma=False)
```
